128 devices in a mesh: grp: 8 (over y, core), sub: 16 (over x, z).
Axes of the slice: x: 4, y: 4, z: 4, core: 2. Of those that a mesh axis runs over, the one named last changes fastest.
Arguments:
- sources: float32 [32, 64, 16384], P(None, None, ('grp', 'sub')), may hold values from -6 to 6
- coords: float32 [3, 64, 16384], P(None, None, ('grp', 'sub')), may hold values from 0 to 2
- leaf_basis: float32 [32, 64, 16384], P(None, None, ('grp', 'sub')), may hold values from -0.75 to 0.75
- transfer: float32 [32, 32, 16384], P(None, None, ('grp', 'sub')), may hold values from -1 to 1
- send_list: int32 [2048, 16], P(('grp', 'sub')), may hold values from 0 to 127
- near_list: int32 [7, 16384], P(None, ('grp', 'sub')), may hold values from 0 to 383
- near_count: int32 [16384], P(('grp', 'sub')), may hold values from 1 to 7, as said below
- far_list: int32 [16, 2048], P(None, ('grp', 'sub')), may hold values from 0 to 255
- coupling: float32 [32, 32, 16, 2048], P(None, None, None, ('grp', 'sub')), may hold values from -0.25 to 0.25
- group_transfer: float32 [32, 32, 2048], P(None, None, ('grp', 'sub')), may hold values from -0.0625 to 0.0625
- group_coupling: float32 [32, 32, 8, 8], replicated, may hold values from -1 to 1
Outputs:
- potential: float32 [32, 64, 16384], P(None, None, ('grp', 'sub'))
The draws below stay inside these ranges and needn't reach their ends.
Inputs may be any that keep to these rules, and one draw needn't show every extreme that they name: `near_count`: every device holds a leaf with 7 live entries; the fewest live entries differ from device to device.
All inputs are finite; a program needn't handle non-finite values.
Results may differ from the reference program's by a relative error of at most 0.0003.
Values sent between devices are 32-bit elements; how exact they have to be, the bound alone decides.
No kernel may reach another device: no remote copies, remote signals or barrier semaphores. Data moves between devices by JAX's collectives and lax.ppermute only.
A program may use at most 192 MiB of HBM per device.

```python
import math
import jax
import jax.numpy as jnp
from jax import lax

LEAF = 64
RHS = 32
RANK = 32
NEAR = 7
FAR = 16
LEAF_DEV = 128
CAP = 16
SLOTS = 384
PAR_GRP = 256
LEAVES = 16384
PARENTS = 2048
N_GRP = 8
N_SUB = 16
DEVICES = 128


def draw_near_count(key, part):
    devices = LEAVES // LEAF_DEV
    first_key = jax.random.fold_in(key, 11)
    second_key = jax.random.fold_in(key, 12)
    lowest = jax.random.randint(first_key, (devices, 1), 1, NEAR)
    counts = jax.random.randint(second_key, (devices, LEAF_DEV), lowest, NEAR + 1)
    counts = counts.at[:, 0].set(NEAR)
    return counts.reshape(-1).astype(jnp.int32)


def set_ends(result, own_key, low, top_value):
    index_at = [jax.random.randint(jax.random.fold_in(own_key, axis), (), 0, length) for axis, length in enumerate(result.shape)]
    widest = result.shape.index(max(result.shape))
    neighbour = index_at[:widest] + [(index_at[widest] + 1) % result.shape[widest]] + index_at[widest + 1:]
    return result.at[tuple(index_at)].set(low).at[tuple(neighbour)].set(top_value)


def block_levels(rng, shape, cuts, smallest, largest):
    gain, own = 1.0, jax.random.fold_in(rng, 6)
    for dim, blocks in cuts:
        heights = jnp.exp(jax.random.uniform(jax.random.fold_in(own, dim), (blocks,), jnp.float32, smallest / len(cuts), largest / len(cuts)))
        gain = gain * jnp.repeat(heights, shape[dim] // blocks).reshape([-1 if axis == dim else 1 for axis in range(len(shape))])
    return gain


def bell_draw(key, extent, scale, bound, cuts=(), kind=jnp.bfloat16):
    values = scale * jax.random.normal(key, extent, jnp.float32)
    if cuts:
        values = values * block_levels(key, extent, cuts, -0.22, 0.18)
    return jnp.clip(values, -bound, bound).astype(kind)


def setup_inputs(seed: int = 0) -> dict:
    keys = jax.random.split(jax.random.key(seed), 12)
    sources = bell_draw(keys[0], (RHS, LEAF, LEAVES), 1.0, 6.0, ((2, 128),), jnp.float32)
    coords = jnp.clip(2.0 * jax.random.uniform(keys[1], (3, LEAF, LEAVES), jnp.float32) ** block_levels(keys[1], (3, LEAF, LEAVES), ((2, 128),), -0.2, 0.2), 0.0, 2.0)
    leaf_basis = bell_draw(keys[2], (RANK, LEAF, LEAVES), LEAF ** -0.5, 0.75, ((2, 128),), jnp.float32)
    transfer = bell_draw(keys[3], (RANK, RANK, LEAVES), RANK ** -0.5, 1.0, ((2, 128),), jnp.float32)
    send_list = set_ends(jax.random.randint(keys[4], (DEVICES * N_SUB, CAP), 0, LEAF_DEV), jax.random.fold_in(keys[4], 1), 0, LEAF_DEV - 1).astype(jnp.int32)
    near_list = set_ends(jax.random.randint(keys[5], (NEAR, LEAVES), 0, SLOTS), jax.random.fold_in(keys[5], 1), 0, SLOTS - 1).astype(jnp.int32)
    near_count = draw_near_count(jax.random.fold_in(keys[11], 71), 0)
    far_list = set_ends(jax.random.randint(keys[7], (FAR, PARENTS), 0, PAR_GRP), jax.random.fold_in(keys[7], 1), 0, PAR_GRP - 1).astype(jnp.int32)
    coupling = bell_draw(keys[8], (RANK, RANK, FAR, PARENTS), (RANK * FAR) ** -0.5, 0.25, ((3, 128),), jnp.float32)
    group_transfer = bell_draw(keys[9], (RANK, RANK, PARENTS), (RANK * PAR_GRP) ** -0.5, 0.0625, ((2, 128),), jnp.float32)
    group_coupling = bell_draw(keys[10], (RANK, RANK, N_GRP, N_GRP), RANK ** -0.5, 1.0, (), jnp.float32)
    return dict(sources=sources, coords=coords, leaf_basis=leaf_basis, transfer=transfer, send_list=send_list, near_list=near_list, near_count=near_count, far_list=far_list, coupling=coupling, group_transfer=group_transfer, group_coupling=group_coupling)


INV_FOUR_PI = 1.0 / (4.0 * math.pi)
EPS_SQ = 0.01
HIGH = lax.Precision.HIGHEST

def near_block(targets, source_pts, source_vals, live):
    offsets = targets[:, :, None, :] - source_pts[:, None, :, :]
    dist_sq = lax.optimization_barrier(jnp.sum(offsets * offsets, axis=0))
    kernel = live.astype(jnp.float32)[None, None, :] * INV_FOUR_PI / jnp.sqrt(dist_sq + EPS_SQ)
    return jnp.einsum('tsl,rsl->rtl', kernel, source_vals, precision=HIGH)

def reference(sources, coords, leaf_basis, transfer, send_list, near_list, near_count, far_list, coupling, group_transfer, group_coupling):
    devices = N_GRP * N_SUB
    leaf_ids = jnp.arange(LEAVES, dtype=jnp.int32)
    owner = leaf_ids // LEAF_DEV
    group_of = owner // N_SUB
    member = owner % N_SUB
    remote = near_list >= LEAF_DEV
    offset = jnp.maximum(near_list - LEAF_DEV, 0)
    sender = group_of[None, :] * N_SUB + offset // CAP
    slot_leaf = send_list[sender * N_SUB + member[None, :], offset % CAP]
    source_leaf = jnp.where(remote, sender * LEAF_DEV + slot_leaf, owner[None, :] * LEAF_DEV + near_list).astype(jnp.int32)

    def near_device(device):
        start = device * LEAF_DEV
        chosen = lax.dynamic_slice_in_dim(source_leaf, start, LEAF_DEV, 1)
        counts = lax.dynamic_slice_in_dim(near_count, start, LEAF_DEV, 0)
        targets = lax.dynamic_slice_in_dim(coords, start, LEAF_DEV, 2)

        def one_entry(entry, total):
            picked = lax.dynamic_index_in_dim(chosen, entry, 0, keepdims=False)
            values = jnp.take(sources, picked, axis=2)
            points = jnp.take(coords, picked, axis=2)
            return total + near_block(targets, points, values, entry < counts)
        return lax.fori_loop(0, NEAR, one_entry, jnp.zeros((RHS, LEAF, LEAF_DEV), jnp.float32))
    stacked = lax.map(near_device, jnp.arange(devices, dtype=jnp.int32))
    near = jnp.transpose(stacked, (1, 2, 0, 3)).reshape(RHS, LEAF, LEAVES)
    skel = jnp.einsum('ktl,rtl->krl', leaf_basis, sources, precision=HIGH)
    lifted = jnp.einsum('jkl,krl->jrl', transfer, skel, precision=HIGH)
    parent_skel = lax.optimization_barrier(jnp.sum(lifted.reshape(RANK, RHS, PARENTS, 8), axis=3))
    parent_group = jnp.arange(PARENTS, dtype=jnp.int32) // PAR_GRP
    partner = (parent_group[None, :] * PAR_GRP + far_list).astype(jnp.int32)
    partners = parent_skel[:, :, partner]
    local_field = jnp.einsum('kjfp,jrfp->krp', coupling, partners, precision=HIGH)
    parts = jnp.einsum('kjp,jrp->krp', group_transfer, parent_skel, precision=HIGH)
    group_skel = lax.optimization_barrier(jnp.sum(parts.reshape(RANK, RHS, N_GRP, PAR_GRP), axis=3))
    others = 1.0 - jnp.eye(N_GRP, dtype=jnp.float32)
    inflow = jnp.einsum('kjgh,jrh->krg', group_coupling * others[None, None, :, :], group_skel, precision=HIGH)
    field = local_field + jnp.einsum('jkp,jrp->krp', group_transfer, inflow[:, :, parent_group], precision=HIGH)
    leaf_field = jnp.einsum('jkl,jrl->krl', transfer, jnp.repeat(field, 8, axis=2), precision=HIGH)
    far = jnp.einsum('ktl,krl->rtl', leaf_basis, leaf_field, precision=HIGH)
    return near + far
```

```python
import functools
import math

import jax
import jax.numpy as jnp
from jax import lax
from jax.experimental import pallas as pl
from jax.experimental.pallas import tpu as pltpu
from jax.sharding import PartitionSpec as P

INV_FOUR_PI = 1.0 / (4.0 * math.pi)
EPS_SQ = 0.01
F32, BF16 = jnp.float32, jnp.bfloat16
NT = (((1,), (1,)), ((), ()))
NN = (((1,), (0,)), ((), ()))

VALS, PARENTS_AT, POINTS_AT, INFLOW_AT, ROWS = 0, 256, 384, 408, 416


def split(x):
    hi = x.astype(BF16)
    return hi, (x - hi.astype(F32)).astype(BF16)


def mm(a, b, dims):
    return lax.dot_general(a, b, dims, preferred_element_type=F32)


def dot3(a, b, dims):
    ah, al = split(a)
    bh, bl = split(b)
    return mm(ah, bh, dims) + (mm(ah, bl, dims) + mm(al, bh, dims))


def low_half(shape):
    return lax.broadcasted_iota(jnp.int32, shape, len(shape) - 1) < 64


def prep_kernel(src, crd, bas, tra, gt, src_t, pts_t, wt, skel, own, w_t):
    def source_row(r, _):
        block = src[r]
        src_t[pl.ds(r, 128, stride=32), :] = jnp.transpose(jnp.concatenate([block, block], 0))
        return 0

    lax.fori_loop(0, 32, source_row, 0)
    for c in range(3):
        block = crd[c]
        pts_t[pl.ds(c, 128, stride=8), :] = jnp.transpose(jnp.concatenate([block, block], 0))

    def w_rows(jb, _):
        acc = [jnp.zeros((64, 128), F32) for _ in range(4)]
        for k in range(32):
            block = bas[k]
            for i in range(4):
                acc[i] = acc[i] + tra[jb * 4 + i, k : k + 1, :] * block
        for i in range(4):
            both = jnp.transpose(jnp.concatenate([acc[i], acc[i]], 0))
            w_t[pl.ds(jb * 4 + i, 128, stride=32), :] = both
        return 0

    lax.fori_loop(0, 8, w_rows, 0)
    low = low_half((32, 128))

    def one_parent(c):
        total = jnp.zeros((64, 64), F32)
        for pair in range(4):
            first, second = [pl.ds(pl.multiple_of((c * 8 + pair * 2 + i) * 32, 32), 32) for i in (0, 1)]
            w = jnp.where(low, w_t[first, :], w_t[second, :])
            s = jnp.where(low, src_t[first, :], src_t[second, :])
            total = total + mm(jnp.concatenate(split(w), 0), jnp.concatenate(split(s), 0), NT)
        both = total[:32] + total[32:]
        return both[:, :32] + both[:, 32:]

    def four_parents(cg, total):
        blocks = [one_parent(cg * 4 + i) for i in range(4)]
        skel[pl.ds(pl.multiple_of(cg * 32, 32), 32), :] = jnp.concatenate(blocks, 1)
        for i in range(4):
            total = total + dot3(gt[:, pl.ds(cg * 4 + i, 1), :].reshape(32, 32), blocks[i], NN)
        return total

    own[...] = jnp.pad(lax.fori_loop(0, 4, four_parents, jnp.zeros((32, 32), F32)), ((0, 0), (0, 96)))

    def w_leaf(l, _):
        rows = pl.ds(pl.multiple_of(l * 32, 32), 32)
        hi, lo = split(w_t[rows, :])
        wt[rows, :] = jnp.where(low, hi.astype(F32), lo.astype(F32)).astype(BF16)
        return 0

    lax.fori_loop(0, 128, w_leaf, 0)


def pack_kernel(send, src_t, pts_t, skel, out):
    low = low_half((32, 128))
    low8 = low_half((8, 128))

    def one_peer(q, _):
        for p in range(8):
            first, second = send[q, 2 * p], send[q, 2 * p + 1]
            rows = [pl.ds(pl.multiple_of(l * 32, 32), 32) for l in (first, second)]
            out[q, pl.ds(VALS + 32 * p, 32), :] = jnp.where(low, src_t[rows[0], :], src_t[rows[1], :])
            rows = [pl.ds(pl.multiple_of(l * 8, 8), 8) for l in (first, second)]
            pts = jnp.where(low8, pts_t[rows[0], :], pts_t[rows[1], :])
            out[q, pl.ds(POINTS_AT + 3 * p, 3), :] = pts[:3]
        out[q, pl.ds(PARENTS_AT, 128), :] = skel[...]
        out[q, pl.ds(INFLOW_AT, 8), :] = jnp.zeros((8, 128), F32)
        return 0

    lax.fori_loop(0, 16, one_peer, 0)


def inflow_kernel(group, row, parts, payload_in, payload, block, sem):
    del payload_in
    total = jnp.zeros((32, 32), F32)
    for h in range(8):
        live = (group[0] != h).astype(F32)
        total = total + dot3(row[:, h, :] * live, parts[h][:, :32], NN)
    block[...] = jnp.concatenate([total[8 * i : 8 * i + 8] for i in range(4)], 1)
    copies = [pltpu.make_async_copy(block, payload.at[q, pl.ds(INFLOW_AT, 8), :], sem.at[q]) for q in range(16)]
    for copy in copies:
        copy.start()
    for copy in copies:
        copy.wait()


def couple_kernel(cpl, out, rows):
    def one_row(k, _):
        for fg in range(4):
            four = jnp.concatenate([cpl[k, 4 * fg + i] for i in range(4)], 1)
            rows[fg, pl.ds(k, 16, stride=32), :] = four
        return 0

    lax.fori_loop(0, 32, one_row, 0)

    def one_parent(c, _):
        at = pl.ds(pl.multiple_of(c * 32, 32), 32)
        hi, lo = split(jnp.concatenate([rows[fg, at, :] for fg in range(4)], 1))
        out[c, 0:32, :] = hi
        out[c, 32:64, :] = lo
        return 0

    lax.fori_loop(0, 16, one_parent, 0)


def final_kernel(
    near, count, far, recv, src_t, pts_own, crd, wt, cpl, gt, out, vals, pts, skel, field, total
):
    low = low_half((32, 128))
    low8 = low_half((8, 128))

    def put(slot, x):
        hi, lo = split(x * INV_FOUR_PI)
        vals[slot, 0:32, :] = hi
        vals[slot, 32:64, :] = lo

    def own_leaf(l, _):
        put(l, src_t[pl.ds(pl.multiple_of(l * 32, 32), 32), :])
        return 0

    lax.fori_loop(0, 128, own_leaf, 0)
    pts[0:1024, :] = pts_own[...]
    vals[384] = jnp.zeros((64, 128), BF16)
    pts[384 * 8 : 385 * 8, :] = jnp.zeros((8, 128), F32)

    def one_sender(s, _):
        for p in range(8):
            slot = 128 + s * 16 + 2 * p
            x = recv[s, pl.ds(VALS + 32 * p, 32), :]
            y = pltpu.roll(x, 64, 1)
            put(slot, jnp.where(low, x, y))
            put(slot + 1, jnp.where(low, y, x))
            x = recv[s, pl.ds(POINTS_AT + 3 * p, 3), :]
            x = jnp.concatenate([x, jnp.zeros((5, 128), F32)], 0)
            y = pltpu.roll(x, 64, 1)
            pts[pl.ds(pl.multiple_of(slot * 8, 8), 8), :] = jnp.where(low8, x, y)
            pts[pl.ds(pl.multiple_of(slot * 8 + 8, 8), 8), :] = jnp.where(low8, y, x)
        for cg in range(4):
            hi, lo = split(recv[s, pl.ds(PARENTS_AT + 32 * cg, 32), :])
            skel[s * 4 + cg, :, 0:128] = hi
            skel[s * 4 + cg, :, 128:256] = lo
        return 0

    lax.fori_loop(0, 16, one_sender, 0)

    packed = recv[0, pl.ds(INFLOW_AT, 8), :]
    for s in range(1, 16):
        packed = packed + recv[s, pl.ds(INFLOW_AT, 8), :]
    inflow = jnp.concatenate([packed[:, 32 * i : 32 * i + 32] for i in range(4)], 0)
    inflow_t = jnp.transpose(jnp.pad(inflow, ((0, 96), (0, 96))))[:32, :32]
    group4 = lax.broadcasted_iota(jnp.int32, (32, 256), 1) // 32 % 4

    def one_parent(c, _):
        acc = jnp.zeros((64, 256), F32)
        for half in range(2):
            blocks = []
            for f in range(8 * half, 8 * half + 8):
                q = far[f, c]
                tile = skel[q // 4]
                blocks.append(jnp.where(group4 == q % 4, tile, jnp.zeros_like(tile)))
            acc = acc + mm(cpl[c, :, 256 * half : 256 * half + 256], jnp.concatenate(blocks, 0), NN)
        both = acc[:32] + acc[32:]
        x = both[:, :128] + both[:, 128:]
        x = x + pltpu.roll(x, 64, 1)
        x = x + pltpu.roll(x, 32, 1)
        x = jnp.transpose(jnp.concatenate([x] * 4, 0))[:32, :32]
        x = x + dot3(inflow_t, gt[:, pl.ds(c, 1), :].reshape(32, 32), NN)
        hi, lo = split(x)
        field[c, 0:32, :] = hi
        field[c, 32:64, :] = lo
        return 0

    lax.fori_loop(0, 16, one_parent, 0)

    def one_leaf(l, _):
        at = jnp.full((64, 128), l, jnp.int32)
        target = [jnp.take_along_axis(crd[c], at, axis=1) for c in range(3)]
        live = count[l]
        acc = mm(field[l // 8], wt[pl.ds(pl.multiple_of(l * 32, 32), 32), :], NN)
        his, los, vs = [], [], []
        for pair in range(4):
            slots = []
            for e in (2 * pair, 2 * pair + 1):
                slots.append(jnp.where(e < live, near[e, l], 384) if e < 7 else 384)
            rows = [pts[pl.ds(pl.multiple_of(s * 8, 8), 8), :] for s in slots]
            source = jnp.where(low8, rows[0], rows[1])
            dist = EPS_SQ
            for c in range(3):
                d = target[c] - source[c : c + 1, :]
                dist = dist + d * d
            hi, lo = split(lax.rsqrt(dist))
            his.append(hi)
            los.append(lo)
            mask = low_half((64, 128))
            vs.append(jnp.where(mask, vals[slots[0]], vals[slots[1]]))
        a = jnp.concatenate([jnp.concatenate(his, 1), jnp.concatenate(los, 1)], 0)
        acc = acc + mm(jnp.concatenate(vs, 1), a, NT)
        total[pl.ds(pl.multiple_of(l * 32, 32), 32), :] = acc[:32] + acc[32:]
        return 0

    lax.fori_loop(0, 128, one_leaf, 0)

    def one_rhs(r, _):
        x = jnp.transpose(total[pl.ds(r, 128, stride=32), :])
        out[r] = x[:64] + x[64:]
        return 0

    lax.fori_loop(0, 32, one_rhs, 0)


VMEM = pl.BlockSpec(memory_space=pltpu.VMEM)
SMEM = pl.BlockSpec(memory_space=pltpu.SMEM)
ANY = pl.BlockSpec(memory_space=pl.ANY)
PARAMS = pltpu.CompilerParams(vmem_limit_bytes=56 << 20)


def f32(*shape):
    return jax.ShapeDtypeStruct(shape, F32)


def body(
    sources,
    coords,
    leaf_basis,
    transfer,
    send_list,
    near_list,
    near_count,
    far_list,
    coupling,
    group_transfer,
    group_coupling,
):
    gt = jnp.transpose(group_transfer, (0, 2, 1))
    src_t, pts_t, wt, skel, own = pl.pallas_call(
        prep_kernel,
        out_shape=(f32(4096, 128), f32(1024, 128), jax.ShapeDtypeStruct((4096, 128), BF16), f32(128, 128), f32(32, 128)),
        in_specs=[VMEM] * 5,
        out_specs=[VMEM] * 5,
        scratch_shapes=[pltpu.VMEM((4096, 128), F32)],
        compiler_params=PARAMS,
        name="prep",
    )(sources, coords, leaf_basis, transfer, gt)
    parts = lax.all_to_all(jnp.broadcast_to(own[None], (8, 32, 128)), "grp", 0, 0, tiled=True)
    payload = pl.pallas_call(
        pack_kernel,
        out_shape=f32(16, ROWS, 128),
        in_specs=[SMEM, VMEM, VMEM, VMEM],
        out_specs=VMEM,
        compiler_params=PARAMS,
        name="pack",
    )(send_list, src_t, pts_t, skel)
    group = lax.axis_index("grp").astype(jnp.int32).reshape(1)
    payload = pl.pallas_call(
        inflow_kernel,
        out_shape=f32(16, ROWS, 128),
        grid_spec=pltpu.PrefetchScalarGridSpec(
            num_scalar_prefetch=1,
            grid=(1,),
            in_specs=[
                pl.BlockSpec((32, pl.Squeezed(), 8, 32), lambda i, g: (0, g[0], 0, 0)),
                pl.BlockSpec((8, 32, 128), lambda i, g: (0, 0, 0)),
                ANY,
            ],
            out_specs=ANY,
            scratch_shapes=[pltpu.VMEM((8, 128), F32), pltpu.SemaphoreType.DMA((16,))],
        ),
        input_output_aliases={3: 0},
        name="inflow",
    )(group, jnp.transpose(group_coupling, (0, 2, 3, 1)), parts, payload)
    recv = lax.all_to_all(payload, "sub", 0, 0, tiled=True)
    cpl = pl.pallas_call(
        couple_kernel,
        out_shape=jax.ShapeDtypeStruct((16, 64, 512), BF16),
        in_specs=[VMEM],
        out_specs=VMEM,
        scratch_shapes=[pltpu.VMEM((4, 512, 128), F32)],
        compiler_params=PARAMS,
        name="couple",
    )(jnp.transpose(coupling, (0, 2, 3, 1)))
    return pl.pallas_call(
        final_kernel,
        out_shape=f32(32, 64, 128),
        in_specs=[SMEM] * 3 + [VMEM] * 7,
        out_specs=VMEM,
        scratch_shapes=[
            pltpu.VMEM((385, 64, 128), BF16),
            pltpu.VMEM((385 * 8, 128), F32),
            pltpu.VMEM((64, 32, 256), BF16),
            pltpu.VMEM((16, 64, 32), BF16),
            pltpu.VMEM((4096, 128), F32),
        ],
        compiler_params=PARAMS,
        name="final",
    )(near_list, near_count, far_list, recv, src_t, pts_t, coords, wt, cpl, gt)


def solution(mesh):
    leaves = P(None, None, ("grp", "sub"))
    return jax.shard_map(
        body,
        mesh=mesh,
        in_specs=(
            leaves,
            leaves,
            leaves,
            leaves,
            P(("grp", "sub"), None),
            P(None, ("grp", "sub")),
            P(("grp", "sub")),
            P(None, ("grp", "sub")),
            P(None, None, None, ("grp", "sub")),
            leaves,
            P(),
        ),
        out_specs=leaves,
        check_vma=False,
    )
```

```python
import math

import jax
import jax.numpy as jnp
from jax import lax
from jax.experimental import pallas as pl
from jax.experimental.pallas import tpu as pltpu
from jax.sharding import PartitionSpec as P

INV_FOUR_PI = 1.0 / (4.0 * math.pi)
EPS_SQ = 0.01
F32, BF16 = jnp.float32, jnp.bfloat16
NT = (((1,), (1,)), ((), ()))
NN = (((1,), (0,)), ((), ()))

POINTS_AT, NEAR_ROWS = 256, 280
INFLOW_AT, FAR_ROWS = 128, 136


def split(x):
    hi = x.astype(BF16)
    return hi, (x - hi.astype(F32)).astype(BF16)


def split3(x):
    hi = x.astype(BF16).astype(F32)
    rest = x - hi
    mid = rest.astype(BF16).astype(F32)
    return hi, mid, rest - mid


def mm(a, b, dims):
    return lax.dot_general(a, b, dims, preferred_element_type=F32)


def dot3(a, b, dims):
    ah, al = split(a)
    bh, bl = split(b)
    return mm(ah, bh, dims) + (mm(ah, bl, dims) + mm(al, bh, dims))


def low_half(shape):
    return lax.broadcasted_iota(jnp.int32, shape, len(shape) - 1) < 64


def rows(i, n):
    return pl.ds(pl.multiple_of(i * n, n), n)


def twice(block):
    return jnp.transpose(jnp.concatenate([block, block], 0))


def pack_kernel(send, src, crd, out, src_t, pts_t, planes):
    def source_rows(i, _):
        for r in range(4):
            planes[i * 4 + r] = twice(src[i * 4 + r])
        return 0

    lax.fori_loop(0, 8, source_rows, 0)

    def eight_leaves(g, _):
        block = jnp.transpose(planes[:, rows(g, 8), :], (1, 0, 2))
        src_t[rows(g, 256), :] = block.reshape(256, 128)
        return 0

    lax.fori_loop(0, 16, eight_leaves, 0)
    for c in range(3):
        planes[c] = twice(crd[c] - 1.0)
    for c in range(3, 8):
        planes[c] = jnp.zeros((128, 128), F32)

    def eight_points(g, _):
        block = jnp.transpose(planes[0:8, rows(g, 8), :], (1, 0, 2))
        pts_t[rows(g, 64), :] = block.reshape(64, 128)
        return 0

    lax.fori_loop(0, 16, eight_points, 0)
    low = low_half((32, 128))
    low8 = low_half((8, 128))

    def one_peer(q, _):
        for p in range(8):
            first, second = send[q, 2 * p], send[q, 2 * p + 1]
            out[q, pl.ds(32 * p, 32), :] = jnp.where(low, src_t[rows(first, 32), :], src_t[rows(second, 32), :])
            pts = jnp.where(low8, pts_t[rows(first, 8), :], pts_t[rows(second, 8), :])
            out[q, pl.ds(POINTS_AT + 3 * p, 3), :] = pts[:3]
        return 0

    lax.fori_loop(0, 16, one_peer, 0)


def upward_kernel(src_t, bas, tra, gt, wt, skel, own, gt_c, planes, w_t):
    gt_c[...] = jnp.transpose(gt[...], (1, 0, 2))

    def w_rows(jb, _):
        acc = [jnp.zeros((64, 128), F32) for _ in range(2)]
        for k in range(32):
            block = bas[k]
            for i in range(2):
                acc[i] = acc[i] + tra[jb * 2 + i, k : k + 1, :] * block
        for i in range(2):
            planes[jb * 2 + i] = twice(acc[i])
        return 0

    lax.fori_loop(0, 16, w_rows, 0)
    low = low_half((256, 128))

    def eight_leaves(g, _):
        block = jnp.transpose(planes[:, rows(g, 8), :], (1, 0, 2)).reshape(256, 128)
        w_t[rows(g, 256), :] = block
        hi = block.astype(BF16).astype(F32)
        wt[rows(g, 256), :] = jnp.where(low, hi, block - hi).astype(BF16)
        return 0

    lax.fori_loop(0, 16, eight_leaves, 0)
    low32 = low_half((32, 128))

    def one_parent(c):
        ws, ss = [], []
        for pair in range(4):
            first, second = [rows(c * 8 + pair * 2 + i, 32) for i in (0, 1)]
            w = jnp.where(low32, w_t[first, :], w_t[second, :])
            s = jnp.where(low32, src_t[first, :], src_t[second, :])
            ws.append(jnp.concatenate(split(w), 0))
            ss.append(jnp.concatenate(split(s), 0))
        total = mm(jnp.concatenate(ws, 1), jnp.concatenate(ss, 1), NT)
        both = total[:32] + total[32:]
        return both[:, :32] + both[:, 32:]

    def four_parents(cg, total):
        blocks = [one_parent(cg * 4 + i) for i in range(4)]
        skel[rows(cg, 32), :] = jnp.concatenate(blocks, 1)
        for i in range(4):
            total = total + dot3(gt_c[cg * 4 + i], blocks[i], NN)
        return total

    total = lax.fori_loop(0, 4, four_parents, jnp.zeros((32, 32), F32))
    own[...] = jnp.concatenate([total[8 * i : 8 * i + 8] for i in range(4)], 1)


def unpack(packed):
    return jnp.concatenate([packed[:, 32 * i : 32 * i + 32] for i in range(4)], 0)


def inflow_kernel(group, row, parts, skel, out):
    total = jnp.zeros((32, 32), F32)
    for m in range(1, 8):
        h = group[0] ^ m
        total = total + dot3(row[:, pl.ds(h, 1), :].reshape(32, 32), unpack(parts[m]), NN)
    packed = jnp.concatenate([total[8 * i : 8 * i + 8] for i in range(4)], 1)
    for q in range(16):
        out[q, 0:128, :] = skel[...]
        out[q, 128:136, :] = packed


def couple_kernel(cpl, out, lines):
    def one_row(k, _):
        for fg in range(4):
            lines[fg, pl.ds(k, 16, stride=32), :] = jnp.concatenate([cpl[k, 4 * fg + i] for i in range(4)], 1)
        return 0

    lax.fori_loop(0, 32, one_row, 0)

    def one_parent(c, _):
        hi, lo = split(jnp.concatenate([lines[fg, rows(c, 32), :] for fg in range(4)], 1))
        out[c, 0:32, :] = hi
        out[c, 32:64, :] = lo
        return 0

    lax.fori_loop(0, 16, one_parent, 0)


def point_rows(x, target):
    line = lax.broadcasted_iota(jnp.int32, x.shape, 0)
    norm = jnp.sum(jnp.where(line < 3, x * x, 0.0), axis=0, keepdims=True)
    if target:
        x = jnp.where(line < 3, -2.0 * x, jnp.where(line == 3, 1.0, jnp.where(line == 4, norm + EPS_SQ, 0.0)))
        a, b, c = split3(x)
        return jnp.concatenate([a, a, b, a, b, c], 0)
    x = jnp.where(line < 3, x, jnp.where(line == 3, norm, jnp.where(line == 4, 1.0, 0.0)))
    a, b, c = split3(x)
    return jnp.concatenate([a, b, a, c, b, a], 0).astype(BF16)


def put_values(ref, slot, x):
    hi, lo = split(x * INV_FOUR_PI)
    ref[slot, 0:32, :] = hi
    ref[slot, 32:64, :] = lo


def own_kernel(src_t, pts_t, vals, feats, targets):
    def some_leaves(i, _):
        for u in range(8):
            l = i * 8 + u
            put_values(vals, l, src_t[rows(l, 32), :])
            x = pts_t[rows(l, 8), :]
            feats[l] = point_rows(x, False)
            targets[l] = jnp.transpose(point_rows(x, True))[:64].astype(BF16)
        return 0

    lax.fori_loop(0, 16, some_leaves, 0)


def near_kernel(near, count, recv, targets, vals_own, feats_own, out, vals, feats, sems):
    copies = [
        pltpu.make_async_copy(vals_own, vals.at[pl.ds(0, 128)], sems.at[0]),
        pltpu.make_async_copy(feats_own, feats.at[pl.ds(0, 128)], sems.at[1]),
    ]
    for copy in copies:
        copy.start()
    vals[384] = jnp.zeros((64, 128), BF16)
    feats[384] = point_rows(jnp.zeros((8, 128), F32), False)
    low = low_half((32, 128))
    low8 = low_half((8, 128))

    def one_sender(s, _):
        for p in range(8):
            slot = 128 + s * 16 + 2 * p
            x = recv[s, pl.ds(32 * p, 32), :]
            y = pltpu.roll(x, 64, 1)
            put_values(vals, slot, jnp.where(low, x, y))
            put_values(vals, slot + 1, jnp.where(low, y, x))
            x = recv[s, pl.ds(POINTS_AT + 3 * p, 3), :]
            x = jnp.concatenate([x, jnp.zeros((5, 128), F32)], 0)
            y = pltpu.roll(x, 64, 1)
            feats[slot] = point_rows(jnp.where(low8, x, y), False)
            feats[slot + 1] = point_rows(jnp.where(low8, y, x), False)
        return 0

    lax.fori_loop(0, 16, one_sender, 0)
    for copy in copies:
        copy.wait()
    mask = low_half((64, 128))
    mask48 = low_half((48, 128))

    def one_leaf(l):
        live = count[l]
        slots = [jnp.where(e < live, near[e, l], 384) if e < 7 else 384 for e in range(8)]
        pairs = [(slots[2 * i], slots[2 * i + 1]) for i in range(4)]
        points = jnp.concatenate([jnp.where(mask48, feats[a], feats[b]) for a, b in pairs], 1)
        values = jnp.concatenate([jnp.where(mask, vals[a], vals[b]) for a, b in pairs], 1)
        kern = lax.rsqrt(mm(targets[l], points, NN))
        acc = mm(values, jnp.concatenate(split(kern), 0), NT)
        out[rows(l, 32), :] = acc[:32] + acc[32:]

    def some_leaves(i, _):
        for u in range(UNROLL):
            one_leaf(i * UNROLL + u)
        return 0

    lax.fori_loop(0, 128 // UNROLL, some_leaves, 0)


UNROLL = 4


def far_kernel(far, recv, cpl, gt_c, wt, near, out, skel, masks, planes):
    def one_sender(s, _):
        for cg in range(4):
            hi, lo = split(recv[s, pl.ds(32 * cg, 32), :])
            skel[s * 4 + cg, :, 0:128] = hi
            skel[s * 4 + cg, :, 128:256] = lo
        return 0

    lax.fori_loop(0, 16, one_sender, 0)
    lane_group = lax.broadcasted_iota(jnp.int32, (32, 256), 1) // 32 % 4
    for i in range(4):
        masks[i] = jnp.where(lane_group == i, 1.0, 0.0).astype(BF16)
    packed = recv[0, pl.ds(INFLOW_AT, 8), :]
    for s in range(1, 16):
        packed = packed + recv[s, pl.ds(INFLOW_AT, 8), :]
    inflow = unpack(packed)
    inflow_t = jnp.transpose(jnp.pad(inflow, ((0, 96), (0, 96))))[:32, :32]

    def one_parent(c):
        blocks = []
        for f in range(16):
            q = far[f, c]
            blocks.append(skel[q >> 2] * masks[q & 3])
        acc = mm(cpl[c], jnp.concatenate(blocks, 0), NN)
        both = acc[:32] + acc[32:]
        x = both[:, :128] + both[:, 128:]
        x = x + pltpu.roll(x, 64, 1)
        x = x + pltpu.roll(x, 32, 1)
        x = jnp.transpose(jnp.concatenate([x] * 4, 0))[:32, :32]
        x = x + dot3(inflow_t, gt_c[c], NN)
        field = jnp.concatenate(split(x), 0)
        leaves = []
        for i in range(8):
            acc = mm(field, wt[rows(c * 8 + i, 32), :], NN)
            leaves.append(acc[:32] + acc[32:] + near[rows(c * 8 + i, 32), :])
        planes[:, rows(c, 8), :] = jnp.transpose(jnp.stack(leaves, 0), (1, 0, 2))

    def some_parents(i, _):
        for u in range(4):
            one_parent(i * 4 + u)
        return 0

    lax.fori_loop(0, 4, some_parents, 0)

    def some_rhs(i, _):
        for u in range(4):
            x = jnp.transpose(planes[i * 4 + u])
            out[i * 4 + u] = x[:64] + x[64:]
        return 0

    lax.fori_loop(0, 8, some_rhs, 0)


VMEM = pl.BlockSpec(memory_space=pltpu.VMEM)
SMEM = pl.BlockSpec(memory_space=pltpu.SMEM)
ANY = pl.BlockSpec(memory_space=pl.ANY)


def f32(*shape):
    return jax.ShapeDtypeStruct(shape, F32)


def b16(*shape):
    return jax.ShapeDtypeStruct(shape, BF16)


def call(kernel, name, out_shape, in_specs, scratch=(), mib=56, **cost):
    several = isinstance(out_shape, tuple)
    return pl.pallas_call(
        kernel,
        out_shape=out_shape,
        in_specs=in_specs,
        out_specs=(VMEM,) * len(out_shape) if several else VMEM,
        scratch_shapes=scratch,
        compiler_params=pltpu.CompilerParams(vmem_limit_bytes=mib << 20),
        cost_estimate=pl.CostEstimate(flops=cost.get("flops", 10**9), bytes_accessed=4 << 20, transcendentals=0),
        name=name,
    )


def body(
    sources,
    coords,
    leaf_basis,
    transfer,
    send_list,
    near_list,
    near_count,
    far_list,
    coupling,
    group_transfer,
    group_coupling,
):
    planes = pltpu.VMEM((32, 128, 128), F32)
    payload, src_t, pts_t = call(
        pack_kernel,
        "pack",
        (f32(16, NEAR_ROWS, 128), f32(4096, 128), f32(1024, 128)),
        [SMEM, VMEM, VMEM],
        [planes],
    )(send_list, sources, coords)
    recv = lax.all_to_all(payload, "sub", 0, 0, tiled=True)
    wt, skel, own, gt_c = call(
        upward_kernel,
        "upward",
        (b16(4096, 128), f32(128, 128), f32(8, 128), f32(16, 32, 32)),
        [VMEM] * 4,
        [planes, pltpu.VMEM((4096, 128), F32)],
    )(src_t, leaf_basis, transfer, jnp.transpose(group_transfer, (0, 2, 1)))
    parts = own[None]
    for step in (1, 2, 4):
        other = lax.ppermute(parts, "grp", [(i, i ^ step) for i in range(8)])
        parts = jnp.concatenate([parts, other], 0)
    group = lax.axis_index("grp").astype(jnp.int32).reshape(1)
    far_payload = pl.pallas_call(
        inflow_kernel,
        out_shape=f32(16, FAR_ROWS, 128),
        grid_spec=pltpu.PrefetchScalarGridSpec(
            num_scalar_prefetch=1,
            grid=(1,),
            in_specs=[
                pl.BlockSpec((32, pl.Squeezed(), 8, 32), lambda i, g: (0, g[0], 0, 0)),
                pl.BlockSpec((8, 8, 128), lambda i, g: (0, 0, 0)),
                pl.BlockSpec((128, 128), lambda i, g: (0, 0)),
            ],
            out_specs=pl.BlockSpec((16, FAR_ROWS, 128), lambda i, g: (0, 0, 0)),
        ),
        name="inflow",
    )(group, jnp.transpose(group_coupling, (0, 2, 3, 1)), parts, skel)
    cpl = call(couple_kernel, "couple", b16(16, 64, 512), [VMEM], [pltpu.VMEM((4, 512, 128), F32)])(
        jnp.transpose(coupling, (0, 2, 3, 1))
    )
    vals_own, feats_own, targets = call(
        own_kernel, "own", (b16(128, 64, 128), b16(128, 48, 128), b16(128, 64, 48)), [VMEM] * 2
    )(src_t, pts_t)
    recv, far_payload, cpl, vals_own, feats_own, targets = lax.optimization_barrier(
        (recv, far_payload, cpl, vals_own, feats_own, targets)
    )
    far_recv = lax.all_to_all(far_payload, "sub", 0, 0, tiled=True)
    near = call(
        near_kernel,
        "near",
        f32(4096, 128),
        [SMEM] * 2 + [VMEM] * 2 + [ANY] * 2,
        [pltpu.VMEM((385, 64, 128), BF16), pltpu.VMEM((385, 48, 128), BF16), pltpu.SemaphoreType.DMA((2,))],
    )(near_list, near_count, recv, targets, vals_own, feats_own)
    return call(
        far_kernel,
        "far",
        f32(32, 64, 128),
        [SMEM] + [VMEM] * 5,
        [pltpu.VMEM((64, 32, 256), BF16), pltpu.VMEM((4, 32, 256), BF16), planes],
    )(far_list, far_recv, cpl, gt_c, wt, near)


def solution(mesh):
    leaves = P(None, None, ("grp", "sub"))
    return jax.shard_map(
        body,
        mesh=mesh,
        in_specs=(
            leaves,
            leaves,
            leaves,
            leaves,
            P(("grp", "sub"), None),
            P(None, ("grp", "sub")),
            P(("grp", "sub")),
            P(None, ("grp", "sub")),
            P(None, None, None, ("grp", "sub")),
            leaves,
            P(),
        ),
        out_specs=leaves,
        check_vma=False,
    )
```

```python
import math

import jax
import jax.numpy as jnp
from jax import lax
from jax.experimental import pallas as pl
from jax.experimental.pallas import tpu as pltpu
from jax.sharding import PartitionSpec as P

INV_FOUR_PI = 1.0 / (4.0 * math.pi)
EPS_SQ = 0.01
F32, BF16 = jnp.float32, jnp.bfloat16
NT = (((1,), (1,)), ((), ()))
NN = (((1,), (0,)), ((), ()))

POINTS_AT, NEAR_ROWS = 256, 280
INFLOW_AT, FAR_ROWS = 128, 136


def split(x):
    hi = x.astype(BF16)
    return hi, (x - hi.astype(F32)).astype(BF16)


def split3(x):
    hi = x.astype(BF16).astype(F32)
    rest = x - hi
    mid = rest.astype(BF16).astype(F32)
    return hi, mid, rest - mid


def mm(a, b, dims):
    return lax.dot_general(a, b, dims, preferred_element_type=F32)


def dot3(a, b, dims):
    ah, al = split(a)
    bh, bl = split(b)
    return mm(ah, bh, dims) + (mm(ah, bl, dims) + mm(al, bh, dims))


def low_half(shape):
    return lax.broadcasted_iota(jnp.int32, shape, len(shape) - 1) < 64


def rows(i, n):
    return pl.ds(pl.multiple_of(i * n, n), n)


def twice(block):
    return jnp.transpose(jnp.concatenate([block, block], 0))


def pack_kernel(send, src, crd, out, src_out, pts_out, src_t, pts_t, planes, blocks, sems):
    def source_rows(i, _):
        for r in range(8):
            planes[i * 8 + r] = twice(src[i * 8 + r])
        return 0

    lax.fori_loop(0, 4, source_rows, 0)

    def eight_leaves(g, _):
        block = jnp.transpose(planes[:, rows(g, 8), :], (1, 0, 2))
        src_t[rows(g, 256), :] = block.reshape(256, 128)
        return 0

    lax.fori_loop(0, 16, eight_leaves, 0)
    for c in range(3):
        planes[c] = twice(crd[c] - 1.0)
    for c in range(3, 8):
        planes[c] = jnp.zeros((128, 128), F32)

    def eight_points(g, _):
        block = jnp.transpose(planes[0:8, rows(g, 8), :], (1, 0, 2))
        pts_t[rows(g, 64), :] = block.reshape(64, 128)
        return 0

    lax.fori_loop(0, 16, eight_points, 0)
    copies = [pltpu.make_async_copy(src_t, src_out, sems.at[16]), pltpu.make_async_copy(pts_t, pts_out, sems.at[17])]
    for copy in copies:
        copy.start()
    low = low_half((32, 128))
    low8 = low_half((8, 128))

    def block_copy(q):
        return pltpu.make_async_copy(blocks.at[q], out.at[q], sems.at[q])

    def one_peer(q, _):
        for p in range(8):
            first, second = send[q, 2 * p], send[q, 2 * p + 1]
            blocks[q, pl.ds(32 * p, 32), :] = jnp.where(low, src_t[rows(first, 32), :], src_t[rows(second, 32), :])
            pts = jnp.where(low8, pts_t[rows(first, 8), :], pts_t[rows(second, 8), :])
            blocks[q, pl.ds(POINTS_AT + 3 * p, 3), :] = pts[:3]
        block_copy(q).start()
        return 0

    lax.fori_loop(0, 16, one_peer, 0)
    for copy in copies + [block_copy(q) for q in range(16)]:
        copy.wait()


def upward_kernel(src_t, bas, tra, gt, wt, skel, own, gt_4, planes, w_t, gt_c):
    gt_c[...] = jnp.transpose(gt[...], (1, 0, 2))
    for i in range(4):
        gt_4[i] = jnp.concatenate([gt_c[4 * i + u] for u in range(4)], 1)

    def w_rows(jb, _):
        acc = [jnp.zeros((64, 128), F32) for _ in range(2)]
        for k in range(32):
            block = bas[k]
            for i in range(2):
                acc[i] = acc[i] + tra[jb * 2 + i, k : k + 1, :] * block
        for i in range(2):
            planes[jb * 2 + i] = twice(acc[i])
        return 0

    lax.fori_loop(0, 16, w_rows, 0)
    low = low_half((256, 128))

    def eight_leaves(g, _):
        block = jnp.transpose(planes[:, rows(g, 8), :], (1, 0, 2)).reshape(256, 128)
        w_t[rows(g, 256), :] = block
        hi = block.astype(BF16).astype(F32)
        wt[rows(g, 256), :] = jnp.where(low, hi, block - hi).astype(BF16)
        return 0

    lax.fori_loop(0, 16, eight_leaves, 0)
    low32 = low_half((32, 128))

    def one_parent(c):
        ws, ss = [], []
        for pair in range(4):
            first, second = [rows(c * 8 + pair * 2 + i, 32) for i in (0, 1)]
            w = jnp.where(low32, w_t[first, :], w_t[second, :])
            s = jnp.where(low32, src_t[first, :], src_t[second, :])
            ws.append(jnp.concatenate(split(w), 0))
            ss.append(jnp.concatenate(split(s), 0))
        total = mm(jnp.concatenate(ws, 1), jnp.concatenate(ss, 1), NT)
        both = total[:32] + total[32:]
        return both[:, :32] + both[:, 32:]

    def four_parents(cg, total):
        blocks = [one_parent(cg * 4 + i) for i in range(4)]
        skel[rows(cg, 32), :] = jnp.concatenate(blocks, 1)
        for i in range(4):
            total = total + dot3(gt_c[cg * 4 + i], blocks[i], NN)
        return total

    total = lax.fori_loop(0, 4, four_parents, jnp.zeros((32, 32), F32))
    own[...] = jnp.concatenate([total[8 * i : 8 * i + 8] for i in range(4)], 1)


def unpack(packed):
    return jnp.concatenate([packed[:, 32 * i : 32 * i + 32] for i in range(4)], 0)


def inflow_kernel(group, row, parts, skel, out):
    total = jnp.zeros((32, 32), F32)
    for m in range(1, 8):
        h = group[0] ^ m
        total = total + dot3(row[:, pl.ds(h, 1), :].reshape(32, 32), unpack(parts[m]), NN)
    packed = jnp.concatenate([total[8 * i : 8 * i + 8] for i in range(4)], 1)
    for q in range(16):
        out[q, 0:128, :] = skel[...]
        out[q, 128:136, :] = packed


def couple_kernel(cpl, lines):
    def some_rows(i, _):
        for u in range(2):
            k = i * 2 + u
            for fg in range(4):
                lines[fg, pl.ds(k, 16, stride=32), :] = jnp.concatenate([cpl[k, 4 * fg + v] for v in range(4)], 1)
        return 0

    lax.fori_loop(0, 16, some_rows, 0)


def point_rows(x, target):
    line = lax.broadcasted_iota(jnp.int32, x.shape, 0)
    norm = jnp.sum(jnp.where(line < 3, x * x, 0.0), axis=0, keepdims=True)
    if target:
        return jnp.where(line < 3, -2.0 * x, jnp.where(line == 3, 1.0, jnp.where(line == 4, norm + EPS_SQ, 0.0)))
    return jnp.where(line < 3, x, jnp.where(line == 3, norm, jnp.where(line == 4, 1.0, 0.0)))


def own_kernel(pts_t, feats, targets):
    def some_leaves(i, _):
        for u in range(8):
            l = i * 8 + u
            x = pts_t[rows(l, 8), :]
            feats[rows(l, 8), :] = point_rows(x, False)
            a, b, c = split3(point_rows(x, True))
            targets[l] = jnp.transpose(jnp.concatenate([a, a, b, a, b, c], 0))[:64].astype(BF16)
        return 0

    lax.fori_loop(0, 16, some_leaves, 0)


def near_kernel(near, count, recv, targets, vals_own, feats_own, out, vals, feats, total, planes, ring_a, ring_b, sems):
    copies = [
        pltpu.make_async_copy(vals_own, vals.at[pl.ds(0, 4096), :], sems.at[0]),
        pltpu.make_async_copy(feats_own, feats.at[pl.ds(0, 1024), :], sems.at[1]),
    ]
    for copy in copies:
        copy.start()
    low = low_half((32, 128))
    low8 = low_half((8, 128))
    vals[pl.ds(384 * 32, 32), :] = jnp.zeros((32, 128), F32)
    feats[pl.ds(384 * 8, 8), :] = point_rows(jnp.zeros((8, 128), F32), False)

    def one_sender(s, _):
        for p in range(8):
            slot = 128 + s * 16 + 2 * p
            x = recv[s, pl.ds(32 * p, 32), :]
            y = pltpu.roll(x, 64, 1)
            vals[rows(slot, 32), :] = jnp.where(low, x, y)
            vals[rows(slot + 1, 32), :] = jnp.where(low, y, x)
            x = recv[s, pl.ds(POINTS_AT + 3 * p, 3), :]
            x = point_rows(jnp.concatenate([x, jnp.zeros((5, 128), F32)], 0), False)
            y = pltpu.roll(x, 64, 1)
            feats[rows(slot, 8), :] = jnp.where(low8, x, y)
            feats[rows(slot + 1, 8), :] = jnp.where(low8, y, x)
        return 0

    lax.fori_loop(0, 16, one_sender, 0)
    for copy in copies:
        copy.wait()

    def pairs_of(l):
        live = count[l]
        slots = [jnp.where(e < live, near[e, l], 384) if e < 7 else 384 for e in range(8)]
        return [(slots[2 * i], slots[2 * i + 1]) for i in range(4)]

    def evaluate(group, ring):
        for u in range(UNROLL):
            l = group * UNROLL + u
            x = [jnp.where(low8, feats[rows(a, 8), :], feats[rows(b, 8), :]) for a, b in pairs_of(l)]
            a, b, c = split3(jnp.concatenate(x, 1))
            points = jnp.concatenate([a, b, a, c, b, a], 0).astype(BF16)
            ring[u] = lax.rsqrt(mm(targets[l], points, NN))

    def multiply(group, ring):
        for u in range(UNROLL):
            l = group * UNROLL + u
            x = [jnp.where(low, vals[rows(a, 32), :], vals[rows(b, 32), :]) for a, b in pairs_of(l)]
            values = jnp.concatenate(split(jnp.concatenate(x, 1)), 0)
            acc = mm(values, jnp.concatenate(split(ring[u]), 0), NT)
            total[rows(l, 32), :] = (acc[:32] + acc[32:]) * INV_FOUR_PI

    groups = 128 // UNROLL
    evaluate(0, ring_a)

    def two_groups(i, _):
        evaluate(2 * i + 1, ring_b)
        multiply(2 * i, ring_a)
        evaluate(jnp.minimum(2 * i + 2, groups - 1), ring_a)
        multiply(2 * i + 1, ring_b)
        return 0

    lax.fori_loop(0, groups // 2, two_groups, 0)

    def eight_leaves(g, _):
        block = total[rows(g, 256), :].reshape(8, 32, 128)
        planes[:, rows(g, 8), :] = jnp.transpose(block, (1, 0, 2))
        return 0

    lax.fori_loop(0, 16, eight_leaves, 0)

    def some_rhs(i, _):
        for u in range(8):
            x = jnp.transpose(planes[i * 8 + u])
            out[i * 8 + u] = x[:64] + x[64:]
        return 0

    lax.fori_loop(0, 4, some_rhs, 0)


UNROLL = 4


def far_kernel(far, recv, cpl, gt_4, wt, near, out, sums, planes):
    lane_group = lax.broadcasted_iota(jnp.int32, (32, 128), 1) // 32

    def one_parent(c):
        blocks = []
        for f in range(16):
            q = far[f, c]
            tile = recv[q >> 4, rows((q >> 2) & 3, 32), :]
            blocks.append(jnp.concatenate(split(jnp.where(lane_group == (q & 3), tile, 0.0)), 1))
        left = jnp.concatenate(split(jnp.concatenate([cpl[i, rows(c, 32), :] for i in range(4)], 1)), 0)
        acc = mm(left, jnp.concatenate(blocks, 0), NN)
        both = acc[:32] + acc[32:]
        x = both[:, :128] + both[:, 128:]
        x = x + pltpu.roll(x, 64, 1)
        sums[rows(c, 32), :] = x + pltpu.roll(x, 32, 1)

    def some_parents(i, _):
        for u in range(4):
            one_parent(i * 4 + u)
        return 0

    lax.fori_loop(0, 4, some_parents, 0)
    packed = recv[0, pl.ds(INFLOW_AT, 8), :]
    for s in range(1, 16):
        packed = packed + recv[s, pl.ds(INFLOW_AT, 8), :]
    inflow_t = jnp.transpose(jnp.pad(unpack(packed), ((0, 96), (0, 96))))[:32, :32]

    def four_parents(i, _):
        x = jnp.transpose(sums[rows(i, 128), :])[:32] + dot3(inflow_t, gt_4[i], NN)
        field = jnp.concatenate(split(x), 0)
        for u in range(4):
            leaves = []
            for v in range(8):
                acc = mm(field[:, 32 * u : 32 * u + 32], wt[rows(i * 32 + u * 8 + v, 32), :], NN)
                leaves.append(acc[:32] + acc[32:])
            planes[:, rows(i * 4 + u, 8), :] = jnp.transpose(jnp.stack(leaves, 0), (1, 0, 2))
        return 0

    lax.fori_loop(0, 4, four_parents, 0)

    def some_rhs(i, _):
        for u in range(8):
            x = jnp.transpose(planes[i * 8 + u])
            out[i * 8 + u] = x[:64] + x[64:] + near[i * 8 + u]
        return 0

    lax.fori_loop(0, 4, some_rhs, 0)


VMEM = pl.BlockSpec(memory_space=pltpu.VMEM)
SMEM = pl.BlockSpec(memory_space=pltpu.SMEM)
ANY = pl.BlockSpec(memory_space=pl.ANY)


def f32(*shape):
    return jax.ShapeDtypeStruct(shape, F32)


def b16(*shape):
    return jax.ShapeDtypeStruct(shape, BF16)


def call(kernel, name, out_shape, in_specs, scratch=(), mib=56, out_specs=None):
    several = isinstance(out_shape, tuple)
    return pl.pallas_call(
        kernel,
        out_shape=out_shape,
        in_specs=in_specs,
        out_specs=out_specs or ((VMEM,) * len(out_shape) if several else VMEM),
        scratch_shapes=scratch,
        compiler_params=pltpu.CompilerParams(vmem_limit_bytes=mib << 20),
        cost_estimate=pl.CostEstimate(flops=10**9, bytes_accessed=4 << 20, transcendentals=0),
        name=name,
    )


def body(
    sources,
    coords,
    leaf_basis,
    transfer,
    send_list,
    near_list,
    near_count,
    far_list,
    coupling,
    group_transfer,
    group_coupling,
):
    planes = pltpu.VMEM((32, 128, 128), F32)
    payload, src_t, pts_t = call(
        pack_kernel,
        "pack",
        (f32(16, NEAR_ROWS, 128), f32(4096, 128), f32(1024, 128)),
        [SMEM, VMEM, VMEM],
        [
            pltpu.VMEM((4096, 128), F32),
            pltpu.VMEM((1024, 128), F32),
            planes,
            pltpu.VMEM((16, NEAR_ROWS, 128), F32),
            pltpu.SemaphoreType.DMA((18,)),
        ],
        out_specs=(ANY,) * 3,
    )(send_list, sources, coords)
    recv = lax.all_to_all(payload, "sub", 0, 0, tiled=True)
    wt, skel, own, gt_4 = call(
        upward_kernel,
        "upward",
        (b16(4096, 128), f32(128, 128), f32(8, 128), f32(4, 32, 128)),
        [VMEM] * 4,
        [planes, pltpu.VMEM((4096, 128), F32), pltpu.VMEM((16, 32, 32), F32)],
    )(src_t, leaf_basis, transfer, jnp.transpose(group_transfer, (0, 2, 1)))
    parts = own[None]
    for step in (1, 2, 4):
        other = lax.ppermute(parts, "grp", [(i, i ^ step) for i in range(8)])
        parts = jnp.concatenate([parts, other], 0)
    group = lax.axis_index("grp").astype(jnp.int32).reshape(1)
    far_payload = pl.pallas_call(
        inflow_kernel,
        out_shape=f32(16, FAR_ROWS, 128),
        grid_spec=pltpu.PrefetchScalarGridSpec(
            num_scalar_prefetch=1,
            grid=(1,),
            in_specs=[
                pl.BlockSpec((32, pl.Squeezed(), 8, 32), lambda i, g: (0, g[0], 0, 0)),
                pl.BlockSpec((8, 8, 128), lambda i, g: (0, 0, 0)),
                pl.BlockSpec((128, 128), lambda i, g: (0, 0)),
            ],
            out_specs=pl.BlockSpec((16, FAR_ROWS, 128), lambda i, g: (0, 0, 0)),
        ),
        name="inflow",
    )(group, jnp.transpose(group_coupling, (0, 2, 3, 1)), parts, skel)
    cpl = call(couple_kernel, "couple", f32(4, 512, 128), [VMEM])(jnp.transpose(coupling, (0, 2, 3, 1)))
    feats, targets = call(own_kernel, "own", (f32(1024, 128), b16(128, 64, 48)), [VMEM])(pts_t)
    recv, far_payload, cpl, feats, targets = lax.optimization_barrier((recv, far_payload, cpl, feats, targets))
    far_recv = lax.all_to_all(far_payload, "sub", 0, 0, tiled=True)
    near = call(
        near_kernel,
        "near",
        f32(32, 64, 128),
        [SMEM] * 2 + [VMEM] * 2 + [ANY] * 2,
        [
            pltpu.VMEM((385 * 32, 128), F32),
            pltpu.VMEM((385 * 8, 128), F32),
            pltpu.VMEM((4096, 128), F32),
            planes,
            pltpu.VMEM((UNROLL, 64, 512), F32),
            pltpu.VMEM((UNROLL, 64, 512), F32),
            pltpu.SemaphoreType.DMA((2,)),
        ],
    )(near_list, near_count, recv, targets, src_t, feats)
    return call(
        far_kernel,
        "far",
        f32(32, 64, 128),
        [SMEM] + [VMEM] * 5,
        [pltpu.VMEM((512, 128), F32), planes],
    )(far_list, far_recv, cpl, gt_4, wt, near)


def solution(mesh):
    leaves = P(None, None, ("grp", "sub"))
    return jax.shard_map(
        body,
        mesh=mesh,
        in_specs=(
            leaves,
            leaves,
            leaves,
            leaves,
            P(("grp", "sub"), None),
            P(None, ("grp", "sub")),
            P(("grp", "sub")),
            P(None, ("grp", "sub")),
            P(None, None, None, ("grp", "sub")),
            leaves,
            P(),
        ),
        out_specs=leaves,
        check_vma=False,
    )
```

```python
import math

import jax
import jax.numpy as jnp
from jax import lax
from jax.experimental import pallas as pl
from jax.experimental.pallas import tpu as pltpu
from jax.sharding import PartitionSpec as P

INV_FOUR_PI = 1.0 / (4.0 * math.pi)
EPS_SQ = 0.01
F32, BF16 = jnp.float32, jnp.bfloat16
NT = (((1,), (1,)), ((), ()))
NN = (((1,), (0,)), ((), ()))

POINTS_AT, NEAR_ROWS = 256, 280
INFLOW_AT, FAR_ROWS = 128, 136


def split(x):
    hi = x.astype(BF16)
    return hi, (x - hi.astype(F32)).astype(BF16)


def split3(x):
    hi = x.astype(BF16).astype(F32)
    rest = x - hi
    mid = rest.astype(BF16).astype(F32)
    return hi, mid, rest - mid


def mm(a, b, dims):
    return lax.dot_general(a, b, dims, preferred_element_type=F32)


def dot3(a, b, dims):
    ah, al = split(a)
    bh, bl = split(b)
    return mm(ah, bh, dims) + (mm(ah, bl, dims) + mm(al, bh, dims))


def low_half(shape):
    return lax.broadcasted_iota(jnp.int32, shape, len(shape) - 1) < 64


def rows(i, n):
    return pl.ds(pl.multiple_of(i * n, n), n)


def twice(block):
    return jnp.transpose(jnp.concatenate([block, block], 0))


def pack_kernel(send, crd, src, out, src_out, pts_out, src_t, pts_t, planes, blocks, sems):
    def source_rows(i, _):
        for r in range(8):
            planes[i * 8 + r] = twice(src[i * 8 + r])
        return 0

    lax.fori_loop(0, 4, source_rows, 0)

    def eight_leaves(i, _):
        for g in (2 * i, 2 * i + 1):
            block = jnp.transpose(planes[:, rows(g, 8), :], (1, 0, 2))
            src_t[rows(g, 256), :] = block.reshape(256, 128)
        return 0

    lax.fori_loop(0, 8, eight_leaves, 0)
    for c in range(3):
        planes[c] = twice(crd[c] - 1.0)
    for c in range(3, 8):
        planes[c] = jnp.zeros((128, 128), F32)

    def eight_points(i, _):
        for u in range(4):
            g = i * 4 + u
            block = jnp.transpose(planes[0:8, rows(g, 8), :], (1, 0, 2))
            pts_t[rows(g, 64), :] = block.reshape(64, 128)
        return 0

    lax.fori_loop(0, 4, eight_points, 0)
    copies = [pltpu.make_async_copy(src_t, src_out, sems.at[16]), pltpu.make_async_copy(pts_t, pts_out, sems.at[17])]
    for copy in copies:
        copy.start()
    low = low_half((32, 128))
    low8 = low_half((8, 128))

    def block_copy(q):
        return pltpu.make_async_copy(blocks.at[q], out.at[q], sems.at[q])

    def two_peers(i, _):
        for q in (2 * i, 2 * i + 1):
            for p in range(8):
                first, second = send[q, 2 * p], send[q, 2 * p + 1]
                blocks[q, pl.ds(32 * p, 32), :] = jnp.where(low, src_t[rows(first, 32), :], src_t[rows(second, 32), :])
                pts = jnp.where(low8, pts_t[rows(first, 8), :], pts_t[rows(second, 8), :])
                blocks[q, pl.ds(POINTS_AT + 3 * p, 3), :] = pts[:3]
            block_copy(q).start()
        return 0

    lax.fori_loop(0, 8, two_peers, 0)
    for copy in copies + [block_copy(q) for q in range(16)]:
        copy.wait()


def upward_kernel(src_t, bas, tra, gt, wt, skel, own, gt_4, planes, w_t, gt_c):
    gt_c[...] = jnp.transpose(gt[...], (1, 0, 2))
    for i in range(4):
        gt_4[i] = jnp.concatenate([gt_c[4 * i + u] for u in range(4)], 1)

    def w_rows(jb, _):
        acc = [jnp.zeros((64, 128), F32) for _ in range(2)]
        for k in range(32):
            block = bas[k]
            for i in range(2):
                acc[i] = acc[i] + tra[jb * 2 + i, k : k + 1, :] * block
        for i in range(2):
            planes[jb * 2 + i] = twice(acc[i])
        return 0

    lax.fori_loop(0, 16, w_rows, 0)
    low = low_half((256, 128))

    def eight_leaves(g, _):
        block = jnp.transpose(planes[:, rows(g, 8), :], (1, 0, 2)).reshape(256, 128)
        w_t[rows(g, 256), :] = block
        hi = block.astype(BF16).astype(F32)
        wt[rows(g, 256), :] = jnp.where(low, hi, block - hi).astype(BF16)
        return 0

    lax.fori_loop(0, 16, eight_leaves, 0)
    low32 = low_half((32, 128))

    def one_parent(c):
        ws, ss = [], []
        for pair in range(4):
            first, second = [rows(c * 8 + pair * 2 + i, 32) for i in (0, 1)]
            w = jnp.where(low32, w_t[first, :], w_t[second, :])
            s = jnp.where(low32, src_t[first, :], src_t[second, :])
            ws.append(jnp.concatenate(split(w), 0))
            ss.append(jnp.concatenate(split(s), 0))
        total = mm(jnp.concatenate(ws, 1), jnp.concatenate(ss, 1), NT)
        both = total[:32] + total[32:]
        return both[:, :32] + both[:, 32:]

    def four_parents(cg, total):
        blocks = [one_parent(cg * 4 + i) for i in range(4)]
        skel[rows(cg, 32), :] = jnp.concatenate(blocks, 1)
        for i in range(4):
            total = total + dot3(gt_c[cg * 4 + i], blocks[i], NN)
        return total

    total = lax.fori_loop(0, 4, four_parents, jnp.zeros((32, 32), F32))
    own[...] = jnp.concatenate([total[8 * i : 8 * i + 8] for i in range(4)], 1)


def unpack(packed):
    return jnp.concatenate([packed[:, 32 * i : 32 * i + 32] for i in range(4)], 0)


def inflow_kernel(group, row, parts, skel, out):
    total = jnp.zeros((32, 32), F32)
    for m in range(1, 8):
        h = group[0] ^ m
        total = total + dot3(row[:, pl.ds(h, 1), :].reshape(32, 32), unpack(parts[m]), NN)
    packed = jnp.concatenate([total[8 * i : 8 * i + 8] for i in range(4)], 1)
    for q in range(16):
        out[q, 0:128, :] = skel[...]
        out[q, 128:136, :] = packed


def couple_kernel(cpl, lines):
    def some_rows(i, _):
        for u in range(2):
            k = i * 2 + u
            for fg in range(4):
                lines[fg, pl.ds(k, 16, stride=32), :] = jnp.concatenate([cpl[k, 4 * fg + v] for v in range(4)], 1)
        return 0

    lax.fori_loop(0, 16, some_rows, 0)


def point_rows(x, target):
    line = lax.broadcasted_iota(jnp.int32, x.shape, 0)
    norm = jnp.sum(jnp.where(line < 3, x * x, 0.0), axis=0, keepdims=True)
    if target:
        return jnp.where(line < 3, -2.0 * x, jnp.where(line == 3, 1.0, jnp.where(line == 4, norm + EPS_SQ, 0.0)))
    return jnp.where(line < 3, x, jnp.where(line == 3, norm, jnp.where(line == 4, 1.0, 0.0)))


def own_kernel(pts_t, feats, targets):
    def some_leaves(i, _):
        for u in range(8):
            l = i * 8 + u
            x = pts_t[rows(l, 8), :]
            feats[rows(l, 8), :] = point_rows(x, False)
            a, b, c = split3(point_rows(x, True))
            targets[l] = jnp.transpose(jnp.concatenate([a, a, b, a, b, c], 0))[:64].astype(BF16)
        return 0

    lax.fori_loop(0, 16, some_leaves, 0)


def near_kernel(
    near, count, recv, targets_in, vals_own, feats_own, out, vals, feats, targets, total, planes, result, ring_a, ring_b, sems
):
    copies = [
        pltpu.make_async_copy(targets_in, targets, sems.at[2]),
        pltpu.make_async_copy(vals_own, vals.at[pl.ds(0, 4096), :], sems.at[0]),
        pltpu.make_async_copy(feats_own, feats.at[pl.ds(0, 1024), :], sems.at[1]),
    ]
    for copy in copies:
        copy.start()
    low = low_half((32, 128))
    low8 = low_half((8, 128))
    vals[pl.ds(384 * 32, 32), :] = jnp.zeros((32, 128), F32)
    feats[pl.ds(384 * 8, 8), :] = point_rows(jnp.zeros((8, 128), F32), False)

    def one_sender(s, _):
        for p in range(8):
            slot = 128 + s * 16 + 2 * p
            x = recv[s, pl.ds(32 * p, 32), :]
            y = pltpu.roll(x, 64, 1)
            vals[rows(slot, 32), :] = jnp.where(low, x, y)
            vals[rows(slot + 1, 32), :] = jnp.where(low, y, x)
            x = recv[s, pl.ds(POINTS_AT + 3 * p, 3), :]
            x = point_rows(jnp.concatenate([x, jnp.zeros((5, 128), F32)], 0), False)
            y = pltpu.roll(x, 64, 1)
            feats[rows(slot, 8), :] = jnp.where(low8, x, y)
            feats[rows(slot + 1, 8), :] = jnp.where(low8, y, x)
        return 0

    lax.fori_loop(0, 16, one_sender, 0)
    for copy in copies:
        copy.wait()

    def pairs_of(l):
        live = count[l]
        slots = [jnp.where(e < live, near[e, l], 384) if e < 7 else 384 for e in range(8)]
        return [(slots[2 * i], slots[2 * i + 1]) for i in range(4)]

    def evaluate(group, ring):
        for u in range(UNROLL):
            l = group * UNROLL + u
            x = [jnp.where(low8, feats[rows(a, 8), :], feats[rows(b, 8), :]) for a, b in pairs_of(l)]
            a, b, c = split3(jnp.concatenate(x, 1))
            points = jnp.concatenate([a, b, a, c, b, a], 0).astype(BF16)
            ring[u] = lax.rsqrt(mm(targets[l], points, NN))

    def multiply(group, ring):
        for u in range(UNROLL):
            l = group * UNROLL + u
            x = [jnp.where(low, vals[rows(a, 32), :], vals[rows(b, 32), :]) for a, b in pairs_of(l)]
            values = jnp.concatenate(split(jnp.concatenate(x, 1)), 0)
            acc = mm(values, jnp.concatenate(split(ring[u]), 0), NT)
            total[rows(l, 32), :] = (acc[:32] + acc[32:]) * INV_FOUR_PI

    groups = 128 // UNROLL
    evaluate(0, ring_a)

    def two_groups(i, _):
        evaluate(2 * i + 1, ring_b)
        multiply(2 * i, ring_a)
        evaluate(jnp.minimum(2 * i + 2, groups - 1), ring_a)
        multiply(2 * i + 1, ring_b)
        return 0

    lax.fori_loop(0, groups // 2, two_groups, 0)

    def eight_leaves(g, _):
        block = total[rows(g, 256), :].reshape(8, 32, 128)
        planes[:, rows(g, 8), :] = jnp.transpose(block, (1, 0, 2))
        return 0

    lax.fori_loop(0, 16, eight_leaves, 0)

    def out_copy(i):
        return pltpu.make_async_copy(result.at[pl.ds(i * 8, 8)], out.at[pl.ds(i * 8, 8)], sems.at[3 + i])

    def some_rhs(i, _):
        for u in range(8):
            x = jnp.transpose(planes[i * 8 + u])
            result[i * 8 + u] = x[:64] + x[64:]
        out_copy(i).start()
        return 0

    lax.fori_loop(0, 4, some_rhs, 0)
    for i in range(4):
        out_copy(i).wait()


UNROLL = 4


def far_kernel(far, recv, gt_4, cpl_in, wt_in, near_in, out, cpl, wt, near, sums, planes, result, sems):
    copies = [
        pltpu.make_async_copy(source, target, sems.at[4 + i])
        for i, (source, target) in enumerate([(cpl_in, cpl), (wt_in, wt), (near_in, near)])
    ]
    for copy in copies:
        copy.start()
    lane_group = lax.broadcasted_iota(jnp.int32, (32, 128), 1) // 32

    def one_parent(c):
        blocks = []
        for f in range(16):
            q = far[f, c]
            tile = recv[q >> 4, rows((q >> 2) & 3, 32), :]
            blocks.append(jnp.concatenate(split(jnp.where(lane_group == (q & 3), tile, 0.0)), 1))
        left = jnp.concatenate(split(jnp.concatenate([cpl[i, rows(c, 32), :] for i in range(4)], 1)), 0)
        acc = mm(left, jnp.concatenate(blocks, 0), NN)
        both = acc[:32] + acc[32:]
        x = both[:, :128] + both[:, 128:]
        x = x + pltpu.roll(x, 64, 1)
        sums[rows(c, 32), :] = x + pltpu.roll(x, 32, 1)

    packed = recv[0, pl.ds(INFLOW_AT, 8), :]
    for s in range(1, 16):
        packed = packed + recv[s, pl.ds(INFLOW_AT, 8), :]
    inflow_t = jnp.transpose(jnp.pad(unpack(packed), ((0, 96), (0, 96))))[:32, :32]

    copies[0].wait()

    def some_parents(i, _):
        for u in range(8):
            one_parent(i * 8 + u)
        return 0

    lax.fori_loop(0, 2, some_parents, 0)
    copies[1].wait()

    def four_parents(i, _):
        x = jnp.transpose(sums[rows(i, 128), :])[:32] + dot3(inflow_t, gt_4[i], NN)
        field = jnp.concatenate(split(x), 0)
        for u in range(4):
            leaves = []
            for v in range(8):
                acc = mm(field[:, 32 * u : 32 * u + 32], wt[rows(i * 32 + u * 8 + v, 32), :], NN)
                leaves.append(acc[:32] + acc[32:])
            planes[:, rows(i * 4 + u, 8), :] = jnp.transpose(jnp.stack(leaves, 0), (1, 0, 2))
        return 0

    lax.fori_loop(0, 4, four_parents, 0)

    copies[2].wait()

    def out_copy(i):
        return pltpu.make_async_copy(result.at[pl.ds(i * 8, 8)], out.at[pl.ds(i * 8, 8)], sems.at[i])

    def some_rhs(i, _):
        for u in range(8):
            x = jnp.transpose(planes[i * 8 + u])
            result[i * 8 + u] = x[:64] + x[64:] + near[i * 8 + u]
        out_copy(i).start()
        return 0

    lax.fori_loop(0, 4, some_rhs, 0)
    for i in range(4):
        out_copy(i).wait()


VMEM = pl.BlockSpec(memory_space=pltpu.VMEM)
SMEM = pl.BlockSpec(memory_space=pltpu.SMEM)
ANY = pl.BlockSpec(memory_space=pl.ANY)
HBM = pl.BlockSpec(memory_space=pltpu.HBM)


def in_hbm(x):
    return pltpu.with_memory_space_constraint(x, pltpu.HBM)


def f32(*shape):
    return jax.ShapeDtypeStruct(shape, F32)


def b16(*shape):
    return jax.ShapeDtypeStruct(shape, BF16)


def call(kernel, name, out_shape, in_specs, scratch=(), mib=56, out_specs=None):
    several = isinstance(out_shape, tuple)
    return pl.pallas_call(
        kernel,
        out_shape=out_shape,
        in_specs=in_specs,
        out_specs=out_specs or ((VMEM,) * len(out_shape) if several else VMEM),
        scratch_shapes=scratch,
        compiler_params=pltpu.CompilerParams(vmem_limit_bytes=mib << 20),
        cost_estimate=pl.CostEstimate(flops=10**9, bytes_accessed=4 << 20, transcendentals=0),
        name=name,
    )


def body(
    sources,
    coords,
    leaf_basis,
    transfer,
    send_list,
    near_list,
    near_count,
    far_list,
    coupling,
    group_transfer,
    group_coupling,
):
    planes = pltpu.VMEM((32, 128, 128), F32)
    payload, src_t, pts_t = call(
        pack_kernel,
        "pack",
        (f32(16, NEAR_ROWS, 128), f32(4096, 128), f32(1024, 128)),
        [SMEM, VMEM, VMEM],
        [
            pltpu.VMEM((4096, 128), F32),
            pltpu.VMEM((1024, 128), F32),
            planes,
            pltpu.VMEM((16, NEAR_ROWS, 128), F32),
            pltpu.SemaphoreType.DMA((18,)),
        ],
        out_specs=(ANY,) * 3,
    )(send_list, coords, sources)
    recv = lax.all_to_all(payload, "sub", 0, 0, tiled=True)
    wt, skel, own, gt_4 = call(
        upward_kernel,
        "upward",
        (b16(4096, 128), f32(128, 128), f32(8, 128), f32(4, 32, 128)),
        [VMEM] * 4,
        [planes, pltpu.VMEM((4096, 128), F32), pltpu.VMEM((16, 32, 32), F32)],
    )(src_t, leaf_basis, transfer, jnp.transpose(group_transfer, (0, 2, 1)))
    parts = own[None]
    for step in (1, 2, 4):
        other = lax.ppermute(parts, "grp", [(i, i ^ step) for i in range(8)])
        parts = jnp.concatenate([parts, other], 0)
    group = lax.axis_index("grp").astype(jnp.int32).reshape(1)
    far_payload = pl.pallas_call(
        inflow_kernel,
        out_shape=f32(16, FAR_ROWS, 128),
        grid_spec=pltpu.PrefetchScalarGridSpec(
            num_scalar_prefetch=1,
            grid=(1,),
            in_specs=[
                pl.BlockSpec((32, pl.Squeezed(), 8, 32), lambda i, g: (0, g[0], 0, 0)),
                pl.BlockSpec((8, 8, 128), lambda i, g: (0, 0, 0)),
                pl.BlockSpec((128, 128), lambda i, g: (0, 0)),
            ],
            out_specs=pl.BlockSpec((16, FAR_ROWS, 128), lambda i, g: (0, 0, 0)),
        ),
        name="inflow",
    )(group, jnp.transpose(group_coupling, (0, 2, 3, 1)), parts, skel)
    cpl = call(couple_kernel, "couple", f32(4, 512, 128), [VMEM])(jnp.transpose(coupling, (0, 2, 3, 1)))
    feats, targets = call(own_kernel, "own", (f32(1024, 128), b16(128, 64, 48)), [VMEM])(pts_t)
    recv, far_payload, cpl, feats, targets = lax.optimization_barrier((recv, far_payload, cpl, feats, targets))
    far_recv = lax.all_to_all(far_payload, "sub", 0, 0, tiled=True)
    near = call(
        near_kernel,
        "near",
        pltpu.HBM((32, 64, 128), F32),
        [SMEM] * 2 + [VMEM] + [HBM] * 3,
        [
            pltpu.VMEM((385 * 32, 128), F32),
            pltpu.VMEM((385 * 8, 128), F32),
            pltpu.VMEM((128, 64, 48), BF16),
            pltpu.VMEM((4096, 128), F32),
            planes,
            pltpu.VMEM((32, 64, 128), F32),
            pltpu.VMEM((UNROLL, 64, 512), F32),
            pltpu.VMEM((UNROLL, 64, 512), F32),
            pltpu.SemaphoreType.DMA((7,)),
        ],
        mib=24,
        out_specs=HBM,
    )(near_list, near_count, recv, *[in_hbm(x) for x in (targets, src_t, feats)])
    return call(
        far_kernel,
        "far",
        f32(32, 64, 128),
        [SMEM] + [VMEM] * 2 + [HBM] * 3,
        [
            pltpu.VMEM((4, 512, 128), F32),
            pltpu.VMEM((4096, 128), BF16),
            pltpu.VMEM((32, 64, 128), F32),
            pltpu.VMEM((512, 128), F32),
            planes,
            pltpu.VMEM((32, 64, 128), F32),
            pltpu.SemaphoreType.DMA((7,)),
        ],
        mib=14,
        out_specs=HBM,
    )(far_list, far_recv, gt_4, *[in_hbm(x) for x in (cpl, wt, near)])


def solution(mesh):
    leaves = P(None, None, ("grp", "sub"))
    return jax.shard_map(
        body,
        mesh=mesh,
        in_specs=(
            leaves,
            leaves,
            leaves,
            leaves,
            P(("grp", "sub"), None),
            P(None, ("grp", "sub")),
            P(("grp", "sub")),
            P(None, ("grp", "sub")),
            P(None, None, None, ("grp", "sub")),
            leaves,
            P(),
        ),
        out_specs=leaves,
        check_vma=False,
    )
```

```python
import math

import jax
import jax.numpy as jnp
from jax import lax
from jax.experimental import pallas as pl
from jax.experimental.pallas import tpu as pltpu
from jax.sharding import PartitionSpec as P

INV_FOUR_PI = 1.0 / (4.0 * math.pi)
EPS_SQ = 0.01
F32, BF16 = jnp.float32, jnp.bfloat16
NT = (((1,), (1,)), ((), ()))
NN = (((1,), (0,)), ((), ()))

POINTS_AT, NEAR_ROWS = 256, 280
INFLOW_AT, FAR_ROWS = 128, 136


def split(x):
    hi = x.astype(BF16)
    return hi, (x - hi.astype(F32)).astype(BF16)


def split3(x):
    hi = x.astype(BF16).astype(F32)
    rest = x - hi
    mid = rest.astype(BF16).astype(F32)
    return hi, mid, rest - mid


def mm(a, b, dims):
    return lax.dot_general(a, b, dims, preferred_element_type=F32)


def dot3(a, b, dims):
    ah, al = split(a)
    bh, bl = split(b)
    return mm(ah, bh, dims) + (mm(ah, bl, dims) + mm(al, bh, dims))


def low_half(shape):
    return lax.broadcasted_iota(jnp.int32, shape, len(shape) - 1) < 64


def rows(i, n):
    return pl.ds(pl.multiple_of(i * n, n), n)


def twice(block):
    return jnp.transpose(jnp.concatenate([block, block], 0))


def pack_kernel(send, crd, src, out, src_out, pts_out, src_t, pts_t, planes, blocks, sems):
    def source_rows(i, _):
        for r in range(8):
            planes[i * 8 + r] = twice(src[i * 8 + r])
        return 0

    lax.fori_loop(0, 4, source_rows, 0)

    def source_copy(i):
        return pltpu.make_async_copy(src_t.at[rows(i, 512), :], src_out.at[rows(i, 512), :], sems.at[17 + i])

    def eight_leaves(i, _):
        for g in (2 * i, 2 * i + 1):
            block = jnp.transpose(planes[:, rows(g, 8), :], (1, 0, 2))
            src_t[rows(g, 256), :] = block.reshape(256, 128)
        source_copy(i).start()
        return 0

    lax.fori_loop(0, 8, eight_leaves, 0)
    for c in range(3):
        planes[c] = twice(crd[c] - 1.0)
    for c in range(3, 8):
        planes[c] = jnp.zeros((128, 128), F32)

    def eight_points(i, _):
        for u in range(4):
            g = i * 4 + u
            block = jnp.transpose(planes[0:8, rows(g, 8), :], (1, 0, 2))
            pts_t[rows(g, 64), :] = block.reshape(64, 128)
        return 0

    lax.fori_loop(0, 4, eight_points, 0)
    points_copy = pltpu.make_async_copy(pts_t, pts_out, sems.at[16])
    points_copy.start()
    low = low_half((32, 128))
    low8 = low_half((8, 128))

    def block_copy(q):
        return pltpu.make_async_copy(blocks.at[q], out.at[q], sems.at[q])

    def two_peers(i, _):
        for q in (2 * i, 2 * i + 1):
            for p in range(8):
                first, second = send[q, 2 * p], send[q, 2 * p + 1]
                blocks[q, pl.ds(32 * p, 32), :] = jnp.where(low, src_t[rows(first, 32), :], src_t[rows(second, 32), :])
                pts = jnp.where(low8, pts_t[rows(first, 8), :], pts_t[rows(second, 8), :])
                blocks[q, pl.ds(POINTS_AT + 3 * p, 3), :] = pts[:3]
            block_copy(q).start()
        return 0

    lax.fori_loop(0, 8, two_peers, 0)
    for copy in [points_copy] + [source_copy(i) for i in range(8)] + [block_copy(q) for q in range(16)]:
        copy.wait()


def upward_kernel(src_t, bas, tra, gt, wt, skel, own, gt_4, planes, w_t, gt_c):
    gt_c[...] = jnp.transpose(gt[...], (1, 0, 2))
    for i in range(4):
        gt_4[i] = jnp.concatenate([gt_c[4 * i + u] for u in range(4)], 1)

    def w_rows(jb, _):
        acc = [jnp.zeros((64, 128), F32) for _ in range(2)]
        for k in range(32):
            block = bas[k]
            for i in range(2):
                acc[i] = acc[i] + tra[jb * 2 + i, k : k + 1, :] * block
        for i in range(2):
            planes[jb * 2 + i] = twice(acc[i])
        return 0

    lax.fori_loop(0, 16, w_rows, 0)
    low = low_half((256, 128))

    def eight_leaves(g, _):
        block = jnp.transpose(planes[:, rows(g, 8), :], (1, 0, 2)).reshape(256, 128)
        w_t[rows(g, 256), :] = block
        hi = block.astype(BF16).astype(F32)
        wt[rows(g, 256), :] = jnp.where(low, hi, block - hi).astype(BF16)
        return 0

    lax.fori_loop(0, 16, eight_leaves, 0)
    low32 = low_half((32, 128))

    def one_parent(c):
        ws, ss = [], []
        for pair in range(4):
            first, second = [rows(c * 8 + pair * 2 + i, 32) for i in (0, 1)]
            w = jnp.where(low32, w_t[first, :], w_t[second, :])
            s = jnp.where(low32, src_t[first, :], src_t[second, :])
            ws.append(jnp.concatenate(split(w), 0))
            ss.append(jnp.concatenate(split(s), 0))
        total = mm(jnp.concatenate(ws, 1), jnp.concatenate(ss, 1), NT)
        both = total[:32] + total[32:]
        return both[:, :32] + both[:, 32:]

    def four_parents(cg, total):
        blocks = [one_parent(cg * 4 + i) for i in range(4)]
        skel[rows(cg, 32), :] = jnp.concatenate(blocks, 1)
        for i in range(4):
            total = total + dot3(gt_c[cg * 4 + i], blocks[i], NN)
        return total

    total = lax.fori_loop(0, 4, four_parents, jnp.zeros((32, 32), F32))
    own[...] = jnp.concatenate([total[8 * i : 8 * i + 8] for i in range(4)], 1)


def unpack(packed):
    return jnp.concatenate([packed[:, 32 * i : 32 * i + 32] for i in range(4)], 0)


def inflow_kernel(group, row, parts, skel, out):
    total = jnp.zeros((32, 32), F32)
    for m in range(1, 8):
        h = group[0] ^ m
        total = total + dot3(row[:, pl.ds(h, 1), :].reshape(32, 32), unpack(parts[m]), NN)
    packed = jnp.concatenate([total[8 * i : 8 * i + 8] for i in range(4)], 1)
    for q in range(16):
        out[q, 0:128, :] = skel[...]
        out[q, 128:136, :] = packed


def couple_kernel(cpl, lines):
    def some_rows(i, _):
        for u in range(2):
            k = i * 2 + u
            for fg in range(4):
                lines[fg, pl.ds(k, 16, stride=32), :] = jnp.concatenate([cpl[k, 4 * fg + v] for v in range(4)], 1)
        return 0

    lax.fori_loop(0, 16, some_rows, 0)


def point_rows(x, target):
    line = lax.broadcasted_iota(jnp.int32, x.shape, 0)
    norm = jnp.sum(jnp.where(line < 3, x * x, 0.0), axis=0, keepdims=True)
    if target:
        return jnp.where(line < 3, -2.0 * x, jnp.where(line == 3, 1.0, jnp.where(line == 4, norm + EPS_SQ, 0.0)))
    return jnp.where(line < 3, x, jnp.where(line == 3, norm, jnp.where(line == 4, 1.0, 0.0)))


def own_kernel(pts_t, feats, targets):
    def some_leaves(i, _):
        for u in range(8):
            l = i * 8 + u
            x = pts_t[rows(l, 8), :]
            feats[rows(l, 8), :] = point_rows(x, False)
            a, b, c = split3(point_rows(x, True))
            targets[l] = jnp.transpose(jnp.concatenate([a, a, b, a, b, c], 0))[:64].astype(BF16)
        return 0

    lax.fori_loop(0, 16, some_leaves, 0)


def near_kernel(
    near, count, recv, targets_in, vals_own, feats_own, out, vals, feats, targets, total, planes, result, ring_a, ring_b, sems
):
    copies = [
        pltpu.make_async_copy(targets_in, targets, sems.at[2]),
        pltpu.make_async_copy(vals_own, vals.at[pl.ds(0, 4096), :], sems.at[0]),
        pltpu.make_async_copy(feats_own, feats.at[pl.ds(0, 1024), :], sems.at[1]),
    ]
    for copy in copies:
        copy.start()
    low = low_half((32, 128))
    low8 = low_half((8, 128))
    vals[pl.ds(384 * 32, 32), :] = jnp.zeros((32, 128), F32)
    feats[pl.ds(384 * 8, 8), :] = point_rows(jnp.zeros((8, 128), F32), False)

    def one_sender(s, _):
        for p in range(8):
            slot = 128 + s * 16 + 2 * p
            x = recv[s, pl.ds(32 * p, 32), :]
            y = pltpu.roll(x, 64, 1)
            vals[rows(slot, 32), :] = jnp.where(low, x, y)
            vals[rows(slot + 1, 32), :] = jnp.where(low, y, x)
            x = recv[s, pl.ds(POINTS_AT + 3 * p, 3), :]
            x = point_rows(jnp.concatenate([x, jnp.zeros((5, 128), F32)], 0), False)
            y = pltpu.roll(x, 64, 1)
            feats[rows(slot, 8), :] = jnp.where(low8, x, y)
            feats[rows(slot + 1, 8), :] = jnp.where(low8, y, x)
        return 0

    lax.fori_loop(0, 16, one_sender, 0)
    for copy in copies:
        copy.wait()

    def pairs_of(l):
        live = count[l]
        slots = [jnp.where(e < live, near[e, l], 384) if e < 7 else 384 for e in range(8)]
        return [(slots[2 * i], slots[2 * i + 1]) for i in range(4)]

    def evaluate(group, ring):
        for u in range(UNROLL):
            l = group * UNROLL + u
            x = [jnp.where(low8, feats[rows(a, 8), :], feats[rows(b, 8), :]) for a, b in pairs_of(l)]
            a, b, c = split3(jnp.concatenate(x, 1))
            points = jnp.concatenate([a, b, a, c, b, a], 0).astype(BF16)
            ring[u] = lax.rsqrt(mm(targets[l], points, NN))

    def multiply(group, ring):
        for u in range(UNROLL):
            l = group * UNROLL + u
            x = [jnp.where(low, vals[rows(a, 32), :], vals[rows(b, 32), :]) for a, b in pairs_of(l)]
            values = jnp.concatenate(split(jnp.concatenate(x, 1)), 0)
            acc = mm(values, jnp.concatenate(split(ring[u]), 0), NT)
            total[rows(l, 32), :] = (acc[:32] + acc[32:]) * INV_FOUR_PI

    groups = 128 // UNROLL
    evaluate(0, ring_a)

    def two_groups(i, _):
        evaluate(2 * i + 1, ring_b)
        multiply(2 * i, ring_a)
        evaluate(jnp.minimum(2 * i + 2, groups - 1), ring_a)
        multiply(2 * i + 1, ring_b)
        return 0

    lax.fori_loop(0, groups // 2, two_groups, 0)

    def eight_leaves(g, _):
        block = total[rows(g, 256), :].reshape(8, 32, 128)
        planes[:, rows(g, 8), :] = jnp.transpose(block, (1, 0, 2))
        return 0

    lax.fori_loop(0, 16, eight_leaves, 0)

    def out_copy(i):
        return pltpu.make_async_copy(result.at[pl.ds(i * 8, 8)], out.at[pl.ds(i * 8, 8)], sems.at[3 + i])

    def some_rhs(i, _):
        for u in range(8):
            x = jnp.transpose(planes[i * 8 + u])
            result[i * 8 + u] = x[:64] + x[64:]
        out_copy(i).start()
        return 0

    lax.fori_loop(0, 4, some_rhs, 0)
    for i in range(4):
        out_copy(i).wait()


UNROLL = 4


def far_kernel(far, recv, gt_4, cpl_in, wt_in, near_in, out, cpl, wt, near, sums, planes, result, sems):
    copies = [
        pltpu.make_async_copy(source, target, sems.at[4 + i])
        for i, (source, target) in enumerate([(cpl_in, cpl), (wt_in, wt), (near_in, near)])
    ]
    copies[0].start()
    lane_group = lax.broadcasted_iota(jnp.int32, (32, 128), 1) // 32

    def one_parent(c):
        blocks = []
        for f in range(16):
            q = far[f, c]
            tile = recv[q >> 4, rows((q >> 2) & 3, 32), :]
            blocks.append(jnp.concatenate(split(jnp.where(lane_group == (q & 3), tile, 0.0)), 1))
        left = jnp.concatenate(split(jnp.concatenate([cpl[i, rows(c, 32), :] for i in range(4)], 1)), 0)
        acc = mm(left, jnp.concatenate(blocks, 0), NN)
        both = acc[:32] + acc[32:]
        x = both[:, :128] + both[:, 128:]
        x = x + pltpu.roll(x, 64, 1)
        sums[rows(c, 32), :] = x + pltpu.roll(x, 32, 1)

    packed = recv[0, pl.ds(INFLOW_AT, 8), :]
    for s in range(1, 16):
        packed = packed + recv[s, pl.ds(INFLOW_AT, 8), :]
    inflow_t = jnp.transpose(jnp.pad(unpack(packed), ((0, 96), (0, 96))))[:32, :32]

    copies[0].wait()
    copies[1].start()
    copies[2].start()

    def some_parents(i, _):
        for u in range(8):
            one_parent(i * 8 + u)
        return 0

    lax.fori_loop(0, 2, some_parents, 0)
    copies[1].wait()

    def four_parents(i, _):
        x = jnp.transpose(sums[rows(i, 128), :])[:32] + dot3(inflow_t, gt_4[i], NN)
        field = jnp.concatenate(split(x), 0)
        for u in range(4):
            leaves = []
            for v in range(0, 8, 2):
                both = [wt[rows(i * 32 + u * 8 + v + w, 32), :] for w in (0, 1)]
                acc = mm(field[:, 32 * u : 32 * u + 32], jnp.concatenate(both, 1), NN)
                acc = acc[:32] + acc[32:]
                leaves += [acc[:, :128], acc[:, 128:]]
            planes[:, rows(i * 4 + u, 8), :] = jnp.transpose(jnp.stack(leaves, 0), (1, 0, 2))
        return 0

    lax.fori_loop(0, 4, four_parents, 0)

    copies[2].wait()

    def out_copy(i):
        return pltpu.make_async_copy(result.at[pl.ds(i * 8, 8)], out.at[pl.ds(i * 8, 8)], sems.at[i])

    def some_rhs(i, _):
        for u in range(8):
            x = jnp.transpose(planes[i * 8 + u])
            result[i * 8 + u] = x[:64] + x[64:] + near[i * 8 + u]
        out_copy(i).start()
        return 0

    lax.fori_loop(0, 4, some_rhs, 0)
    for i in range(4):
        out_copy(i).wait()


VMEM = pl.BlockSpec(memory_space=pltpu.VMEM)
SMEM = pl.BlockSpec(memory_space=pltpu.SMEM)
ANY = pl.BlockSpec(memory_space=pl.ANY)
HBM = pl.BlockSpec(memory_space=pltpu.HBM)


def in_hbm(x):
    return pltpu.with_memory_space_constraint(x, pltpu.HBM)


def f32(*shape):
    return jax.ShapeDtypeStruct(shape, F32)


def b16(*shape):
    return jax.ShapeDtypeStruct(shape, BF16)


def call(kernel, name, out_shape, in_specs, scratch=(), mib=56, out_specs=None):
    several = isinstance(out_shape, tuple)
    return pl.pallas_call(
        kernel,
        out_shape=out_shape,
        in_specs=in_specs,
        out_specs=out_specs or ((VMEM,) * len(out_shape) if several else VMEM),
        scratch_shapes=scratch,
        compiler_params=pltpu.CompilerParams(vmem_limit_bytes=mib << 20),
        cost_estimate=pl.CostEstimate(flops=10**9, bytes_accessed=4 << 20, transcendentals=0),
        name=name,
    )


def body(
    sources,
    coords,
    leaf_basis,
    transfer,
    send_list,
    near_list,
    near_count,
    far_list,
    coupling,
    group_transfer,
    group_coupling,
):
    planes = pltpu.VMEM((32, 128, 128), F32)
    payload, src_t, pts_t = call(
        pack_kernel,
        "pack",
        (f32(16, NEAR_ROWS, 128), f32(4096, 128), f32(1024, 128)),
        [SMEM, VMEM, VMEM],
        [
            pltpu.VMEM((4096, 128), F32),
            pltpu.VMEM((1024, 128), F32),
            planes,
            pltpu.VMEM((16, NEAR_ROWS, 128), F32),
            pltpu.SemaphoreType.DMA((25,)),
        ],
        out_specs=(ANY,) * 3,
    )(send_list, coords, sources)
    recv = lax.all_to_all(payload, "sub", 0, 0, tiled=True)
    wt, skel, own, gt_4 = call(
        upward_kernel,
        "upward",
        (b16(4096, 128), f32(128, 128), f32(8, 128), f32(4, 32, 128)),
        [VMEM] * 4,
        [planes, pltpu.VMEM((4096, 128), F32), pltpu.VMEM((16, 32, 32), F32)],
    )(src_t, leaf_basis, transfer, jnp.transpose(group_transfer, (0, 2, 1)))
    parts = own[None]
    for step in (1, 2, 4):
        other = lax.ppermute(parts, "grp", [(i, i ^ step) for i in range(8)])
        parts = jnp.concatenate([parts, other], 0)
    group = lax.axis_index("grp").astype(jnp.int32).reshape(1)
    far_payload = pl.pallas_call(
        inflow_kernel,
        out_shape=f32(16, FAR_ROWS, 128),
        grid_spec=pltpu.PrefetchScalarGridSpec(
            num_scalar_prefetch=1,
            grid=(1,),
            in_specs=[
                pl.BlockSpec((32, pl.Squeezed(), 8, 32), lambda i, g: (0, g[0], 0, 0)),
                pl.BlockSpec((8, 8, 128), lambda i, g: (0, 0, 0)),
                pl.BlockSpec((128, 128), lambda i, g: (0, 0)),
            ],
            out_specs=pl.BlockSpec((16, FAR_ROWS, 128), lambda i, g: (0, 0, 0)),
        ),
        name="inflow",
    )(group, jnp.transpose(group_coupling, (0, 2, 3, 1)), parts, skel)
    cpl = call(couple_kernel, "couple", f32(4, 512, 128), [VMEM])(jnp.transpose(coupling, (0, 2, 3, 1)))
    feats, targets = call(own_kernel, "own", (f32(1024, 128), b16(128, 64, 48)), [VMEM])(pts_t)
    recv, far_payload, cpl, feats, targets = lax.optimization_barrier((recv, far_payload, cpl, feats, targets))
    far_recv = lax.all_to_all(far_payload, "sub", 0, 0, tiled=True)
    near = call(
        near_kernel,
        "near",
        pltpu.HBM((32, 64, 128), F32),
        [SMEM] * 2 + [VMEM] + [HBM] * 3,
        [
            pltpu.VMEM((385 * 32, 128), F32),
            pltpu.VMEM((385 * 8, 128), F32),
            pltpu.VMEM((128, 64, 48), BF16),
            pltpu.VMEM((4096, 128), F32),
            planes,
            pltpu.VMEM((32, 64, 128), F32),
            pltpu.VMEM((UNROLL, 64, 512), F32),
            pltpu.VMEM((UNROLL, 64, 512), F32),
            pltpu.SemaphoreType.DMA((7,)),
        ],
        mib=24,
        out_specs=HBM,
    )(near_list, near_count, recv, *[in_hbm(x) for x in (targets, src_t, feats)])
    return call(
        far_kernel,
        "far",
        f32(32, 64, 128),
        [SMEM] + [VMEM] * 2 + [HBM] * 3,
        [
            pltpu.VMEM((4, 512, 128), F32),
            pltpu.VMEM((4096, 128), BF16),
            pltpu.VMEM((32, 64, 128), F32),
            pltpu.VMEM((512, 128), F32),
            planes,
            pltpu.VMEM((32, 64, 128), F32),
            pltpu.SemaphoreType.DMA((7,)),
        ],
        mib=14,
        out_specs=HBM,
    )(far_list, far_recv, gt_4, *[in_hbm(x) for x in (cpl, wt, near)])


def solution(mesh):
    leaves = P(None, None, ("grp", "sub"))
    return jax.shard_map(
        body,
        mesh=mesh,
        in_specs=(
            leaves,
            leaves,
            leaves,
            leaves,
            P(("grp", "sub"), None),
            P(None, ("grp", "sub")),
            P(("grp", "sub")),
            P(None, ("grp", "sub")),
            P(None, None, None, ("grp", "sub")),
            leaves,
            P(),
        ),
        out_specs=leaves,
        check_vma=False,
    )
```
